128 devices in a mesh: exp: 32 (over z, x_lo, y), row: 4 (over x_hi, core).
Axes of the slice: x: 4 (x_hi: 2, x_lo: 2; x = x_hi * 2 + x_lo), y: 4, z: 4, core: 2. Of those that a mesh axis runs over, the one named last changes fastest.
Arguments:
- latent: bfloat16 [4, 1024, 1024], P(None, 'row', 'exp'), may hold values from -6 to 6
- row_taps: bfloat16 [16, 21], replicated, may hold values from -1.25 to 1.25
- column_taps: bfloat16 [16, 21], replicated, may hold values from -1.25 to 1.25
- coefficients: bfloat16 [32, 16, 1024, 1024], P('exp', None, 'row'), may hold values from -1.5 to 1.5
- observed: bfloat16 [32, 1024, 1024], P('exp', 'row'), may hold values from -6 to 6
- cell_of: int32 [32, 1], replicated, may hold values from 0 to 3
- valid_rows: int32 [32, 1024], P('exp', 'row'), may hold values 0 or 1
Outputs:
- gradient: float32 [4, 1024, 1024], P(None, 'row', 'exp')
- residuals: float32 [32, 1024, 1024], P('exp', 'row')
The draws below stay inside these ranges and needn't reach their ends.
Inputs may be any that keep to these rules, and one draw needn't show every extreme that they name: `cell_of`: every sky cell is covered by at least one exposure.
All inputs are finite; a program needn't handle non-finite values. No bound on the sum of `valid_rows` on one device may be relied on, other than what follows from the above.
Results may differ from the reference program's by a relative error of at most 0.0023.
Values may be sent and summed in bfloat16 or wider, within the bound.
No kernel may reach another device: no remote copies, remote signals or barrier semaphores. Data moves between devices by JAX's collectives and lax.ppermute only.
A program may use at most 128 MiB of HBM per device.

```python
import jax
import jax.numpy as jnp
from jax import lax

KERNELS = 16
TAPS = 21
CELLS = 4
COLS = 1024
CELL_ROWS = 1024
EXPOSURES = 32


def with_ends(drawn, stream_key, low, top_value):
    spot = [jax.random.randint(jax.random.fold_in(stream_key, axis), (), 0, length) for axis, length in enumerate(drawn.shape)]
    main_axis = drawn.shape.index(max(drawn.shape))
    neighbour = spot[:main_axis] + [(spot[main_axis] + 1) % drawn.shape[main_axis]] + spot[main_axis + 1:]
    return drawn.at[tuple(spot)].set(low).at[tuple(neighbour)].set(top_value)


def shard_levels(rng, extent, cuts, low, high):
    loudness, own = 1.0, jax.random.fold_in(rng, 6)
    for axis_at, blocks in cuts:
        steps = jnp.exp(jax.random.uniform(jax.random.fold_in(own, axis_at), (blocks,), jnp.float32, low / len(cuts), high / len(cuts)))
        loudness = loudness * jnp.repeat(steps, extent[axis_at] // blocks).reshape([-1 if axis == axis_at else 1 for axis in range(len(extent))])
    return loudness


def choose_distinct(rng, rows, number_of, top, lift):
    ranking = jax.random.permutation(jax.random.fold_in(rng, 1), number_of)
    pull = ranking
    for power in range(3):
        pull = pull * pull // number_of
    pull = pull * lift // number_of
    chance = jax.random.randint(jax.random.fold_in(rng, 2), (rows, number_of), 0, 4096) + pull
    sure = jax.random.permutation(jax.random.fold_in(rng, 3), rows)[jnp.arange(number_of) % rows]
    chance = jnp.where(jnp.arange(rows)[:, None] == sure[None, :], 1 << 14, chance)
    priority = chance * number_of + jnp.arange(number_of)
    return lax.top_k(priority.astype(jnp.int32), top)[1].astype(jnp.int32)


def gaussian(own_key, shape, spread, reach, shards=(), held_as=jnp.bfloat16):
    drawn = jax.random.normal(own_key, shape, jnp.float32) * spread
    if len(shards) > 0:
        drawn = shard_levels(own_key, shape, shards, -0.22, 0.18) * drawn
    return jnp.clip(drawn, min=-reach, max=reach).astype(held_as)


def setup_inputs(seed: int = 0) -> dict:
    key_of = jax.random.split(jax.random.key(seed), 8)
    return {
        "latent": gaussian(key_of[0], (CELLS, CELL_ROWS, COLS), 1.0, 6.0, ((1, 4), (2, 32))),
        "row_taps": gaussian(key_of[1], (KERNELS, TAPS), TAPS ** -0.5, 1.25),
        "column_taps": gaussian(key_of[2], (KERNELS, TAPS), TAPS ** -0.5, 1.25),
        "coefficients": gaussian(key_of[3], (EXPOSURES, KERNELS, CELL_ROWS, COLS), 0.25, 1.5, ((0, 32), (2, 4))),
        "observed": gaussian(key_of[4], (EXPOSURES, CELL_ROWS, COLS), 1.0, 6.0, ((0, 32), (1, 4))),
        "cell_of": choose_distinct(key_of[5], EXPOSURES, CELLS, 1, 2048),
        "valid_rows": with_ends((jax.random.randint(key_of[6], (EXPOSURES, CELL_ROWS), 0, 8) < 7).astype(jnp.int32), jax.random.fold_in(key_of[6], 1), 0, 1),
    }


def bands(kernel_taps, adjoint):
    tap_count = kernel_taps.shape[1]
    halfwidth = tap_count // 2
    inputs_at = jnp.arange(384)[:, None]
    outputs_at = jnp.arange(128)[None, :]
    if adjoint:
        offset = outputs_at - inputs_at + 128 + halfwidth
    else:
        offset = inputs_at - 128 - outputs_at + halfwidth
    onehot = (offset[:, :, None] == jnp.arange(tap_count)[None, None, :]).astype(jnp.float32)
    return jnp.einsum('kt,pqt->kpq', kernel_taps.astype(jnp.float32), onehot)


def stacked_blocks(source):
    length = source.shape[-1]
    nblocks = length // 128
    padding = [(0, 0)] * (source.ndim - 1) + [(128, 128)]
    padded = jnp.pad(source, padding)
    blocked = padded.reshape(source.shape[:-1] + (nblocks + 2, 128))
    return jnp.concatenate([blocked[..., :-2, :], blocked[..., 1:-1, :], blocked[..., 2:, :]], axis=-1)


def filter_last(source, band_table):
    stacked = stacked_blocks(source)
    result = jnp.einsum('kabp,kpq->kabq', stacked, band_table)
    return result.reshape(source.shape)


def reference(latent, row_taps, column_taps, coefficients, observed, cell_of, valid_rows):
    forward_row = bands(row_taps, False)
    forward_col = bands(column_taps, False)
    adjoint_row = bands(row_taps, True)
    adjoint_col = bands(column_taps, True)
    kernel_count = row_taps.shape[0]
    cell_count = latent.shape[0]

    def blur_cell(image):
        stacked = stacked_blocks(image.astype(jnp.float32))
        result = jnp.einsum('abp,kpq->kabq', stacked, forward_row)
        return result.reshape((kernel_count,) + image.shape).astype(jnp.bfloat16)

    rowblur = lax.map(blur_cell, latent)

    def one_exposure(total, inputs):
        coeffs, seen, cell, usable = inputs
        blurred = lax.dynamic_index_in_dim(rowblur, cell, 0, keepdims=False).astype(jnp.float32)
        vertical = jnp.swapaxes(filter_last(jnp.swapaxes(blurred, 1, 2), forward_col), 1, 2)
        predicted = jnp.sum(coeffs.astype(jnp.float32) * vertical, axis=0)
        residual = usable.astype(jnp.float32)[:, None] * (predicted - seen.astype(jnp.float32))
        weighted = lax.optimization_barrier((coeffs.astype(jnp.float32) * residual[None]).astype(jnp.bfloat16))
        colback = jnp.swapaxes(filter_last(jnp.swapaxes(weighted.astype(jnp.float32), 1, 2), adjoint_col), 1, 2)
        colback = lax.optimization_barrier(colback.astype(jnp.bfloat16))
        stacked = stacked_blocks(colback.astype(jnp.float32))
        own_term = jnp.einsum('kabp,kpq->abq', stacked, adjoint_row).reshape(residual.shape)
        selector = (jnp.arange(cell_count) == cell).astype(jnp.float32)
        total = total + selector[:, None, None] * own_term[None]
        return total, residual

    start = jnp.zeros(latent.shape, jnp.float32)
    gradient, residuals = lax.scan(one_exposure, start, (coefficients, observed, cell_of[:, 0].astype(jnp.int32), valid_rows))
    return gradient, residuals
```

```python
import jax
import jax.numpy as jnp
from jax import lax
from jax.experimental import pallas as pl
from jax.experimental.pallas import tpu as pltpu
from jax.sharding import PartitionSpec as P

F32 = jnp.float32
BF16 = jnp.bfloat16
KERNELS = 16
PAIRS = KERNELS // 2
TAPS = 21
HALF = TAPS // 2
CELLS = 4
EXPOSURES = 32
ROWS = 256
COLS = 1024
BLOCKS = COLS // 128
OWN = COLS // EXPOSURES
SKY = 32
RIM = 16
LAT = ROWS + 2 * SKY
LATP = 384
EXT = ROWS + 2 * RIM
HOUT = EXT // 2
RBR = HOUT + 256
WR = 384

VMEM = pl.BlockSpec(memory_space=pltpu.VMEM)
SMEM = pl.BlockSpec(memory_space=pltpu.SMEM)
ANY = pl.BlockSpec(memory_space=pl.ANY)


def dot(a, b):
    return lax.dot_general(a, b, (((1,), (0,)), ((), ())), preferred_element_type=F32)


def dot_nt(a, b):
    return lax.dot_general(a, b, (((1,), (1,)), ((), ())), preferred_element_type=F32)


def base_rows(taps, place):
    lane = lax.broadcasted_iota(jnp.int32, (KERNELS, 256), 1)
    out = jnp.zeros((KERNELS, 256), F32)
    for t in range(TAPS):
        out = jnp.where(lane == place(t) % 256, taps[:, t : t + 1], out)
    return out


def skewed(row, count):
    return pltpu.roll(jnp.broadcast_to(row, (count, 256)), 0, 1, stride=1, stride_axis=0).astype(BF16)


def column_of(valid):
    return jnp.broadcast_to(valid, (128, valid.shape[1])).T


def prepare_kernel(row_ref, col_ref, valid_ref, obs_ref, coef_hbm, f_ref, c_ref, a_ref, b_ref, up_ref, down_ref, head, tail, sem):
    head_in = pltpu.make_async_copy(coef_hbm.at[0, :, pl.ds(0, RIM), :], head, sem.at[0])
    tail_in = pltpu.make_async_copy(coef_hbm.at[0, :, pl.ds(ROWS - RIM, RIM), :], tail, sem.at[1])
    head_in.start()
    tail_in.start()
    rows = row_ref[...].astype(F32)
    cols = col_ref[...].astype(F32)
    f_base = base_rows(rows, lambda t: t - HALF)
    b_base = base_rows(rows, lambda t: HALF - t)
    c_base = base_rows(cols, lambda t: t + SKY - RIM - HALF)
    a_base = base_rows(cols, lambda t: RIM + HALF - t)
    for k in range(KERNELS):
        i, q = k // 2, k % 2
        f_ref[i, 128 * q : 128 * q + 128, :] = skewed(f_base[k : k + 1], 128)
        b_ref[i, :, 256 * q : 256 * q + 256] = skewed(b_base[k : k + 1], 128)
        c_ref[k] = skewed(c_base[k : k + 1], HOUT)
        a_ref[k] = skewed(a_base[k : k + 1], 128)
    mask = column_of(valid_ref[...].astype(F32))
    head_mask = jnp.concatenate([mask[:RIM]] * BLOCKS, axis=1)
    tail_mask = jnp.concatenate([mask[ROWS - RIM :]] * BLOCKS, axis=1)
    up_ref[KERNELS] = (obs_ref[0, :RIM, :].astype(F32) * head_mask).astype(BF16)
    down_ref[KERNELS] = (obs_ref[0, ROWS - RIM :, :].astype(F32) * tail_mask).astype(BF16)
    head_in.wait()
    tail_in.wait()
    for k in range(KERNELS):
        up_ref[k] = (head[k].astype(F32) * head_mask).astype(BF16)
        down_ref[k] = (tail[k].astype(F32) * tail_mask).astype(BF16)


def prepare(row_taps, column_taps, valid, observed, coefficients):
    rim = jax.ShapeDtypeStruct((KERNELS + 1, RIM, COLS), BF16)
    return pl.pallas_call(
        prepare_kernel,
        out_shape=(
            jax.ShapeDtypeStruct((PAIRS, 256, 256), BF16),
            jax.ShapeDtypeStruct((KERNELS, HOUT, 256), BF16),
            jax.ShapeDtypeStruct((KERNELS, 128, 256), BF16),
            jax.ShapeDtypeStruct((PAIRS, 128, 512), BF16),
            rim,
            rim,
        ),
        in_specs=[VMEM, VMEM, VMEM, VMEM, ANY],
        out_specs=(VMEM,) * 6,
        scratch_shapes=[
            pltpu.VMEM((KERNELS, RIM, COLS), BF16),
            pltpu.VMEM((KERNELS, RIM, COLS), BF16),
            pltpu.SemaphoreType.DMA((2,)),
        ],
        name="prepare",
    )(row_taps, column_taps, valid, observed, coefficients)


def pack_kernel(cell_ref, lat_ref, above_ref, below_ref, out_ref, turned):
    eye = (
        lax.broadcasted_iota(jnp.int32, (OWN, OWN), 0) == lax.broadcasted_iota(jnp.int32, (OWN, OWN), 1)
    ).astype(BF16)
    for c in range(CELLS):
        turned[c, :, 0:SKY] = dot_nt(eye, above_ref[c]).astype(BF16)
        turned[c, :, SKY : SKY + ROWS] = dot_nt(eye, lat_ref[c]).astype(BF16)
        turned[c, :, SKY + ROWS : LAT] = dot_nt(eye, below_ref[c]).astype(BF16)
        turned[c, :, LAT:] = jnp.zeros((OWN, LATP - LAT), BF16)
    for e in range(EXPOSURES):
        out_ref[e] = turned[cell_ref[e, 0]]


def pack(cell_of, latent, above, below):
    return pl.pallas_call(
        pack_kernel,
        out_shape=jax.ShapeDtypeStruct((EXPOSURES, OWN, LATP), BF16),
        in_specs=[SMEM, VMEM, VMEM, VMEM],
        out_specs=VMEM,
        scratch_shapes=[pltpu.VMEM((CELLS, OWN, LATP), BF16)],
        name="pack",
    )(cell_of, latent, above, below)


def main_kernel(
    strip_ref, valid_ref, f_ref, c_ref, a_ref, b_ref, coef_hbm, obs_hbm, above_hbm, below_hbm,
    res_hbm, send_ref,
    sky, windows, coef, obs, rb, pred, w, cb, acc, sem,
):
    def coef_in(k):
        return pltpu.make_async_copy(coef_hbm.at[0, k], coef.at[k, pl.ds(RIM, ROWS), :], sem.at[k])

    rims = [
        pltpu.make_async_copy(obs_hbm.at[0], obs.at[pl.ds(RIM, ROWS), :], sem.at[KERNELS]),
        pltpu.make_async_copy(above_hbm.at[KERNELS], obs.at[pl.ds(0, RIM), :], sem.at[KERNELS + 1]),
        pltpu.make_async_copy(below_hbm.at[KERNELS], obs.at[pl.ds(RIM + ROWS, RIM), :], sem.at[KERNELS + 2]),
        pltpu.make_async_copy(above_hbm.at[pl.ds(0, KERNELS)], coef.at[:, pl.ds(0, RIM), :], sem.at[KERNELS + 3]),
        pltpu.make_async_copy(
            below_hbm.at[pl.ds(0, KERNELS)], coef.at[:, pl.ds(RIM + ROWS, RIM), :], sem.at[KERNELS + 4]
        ),
    ]
    for copy in rims:
        copy.start()
    for k in range(KERNELS):
        coef_in(k).start()

    low = lax.broadcasted_iota(jnp.int32, (LAT, 128), 1) < 64
    for j in range(BLOCKS):
        sky[j] = strip_ref[128 * j : 128 * j + 128, :].astype(F32).T[:LAT]
    zero = jnp.zeros((LAT, 128), F32)
    for j in range(BLOCKS):
        after = sky[j + 1] if j + 1 < BLOCKS else zero
        before = sky[j - 1] if j > 0 else zero
        windows[j, :, 0:128] = sky[j].astype(BF16)
        windows[j, :, 128:256] = jnp.where(low, after, before).astype(BF16)
    rb[:, LAT:, :] = jnp.zeros((2, RBR - LAT, COLS), BF16)
    w[:, EXT:, :] = jnp.zeros((2, WR - EXT, COLS), BF16)
    for copy in rims:
        copy.wait()
    pred[...] = -obs[...].astype(F32)

    def forward(i, carry):
        f = f_ref[i]
        for j in range(BLOCKS):
            both = dot_nt(windows[j], f)
            rb[0, 0:LAT, 128 * j : 128 * j + 128] = both[:, :128].astype(BF16)
            rb[1, 0:LAT, 128 * j : 128 * j + 128] = both[:, 128:].astype(BF16)
        for q in range(2):
            k = 2 * i + q
            coef_in(k).wait()
            c = c_ref[k]
            for h in range(2):
                out = slice(HOUT * h, HOUT * h + HOUT)
                for x in range(0, COLS, 256):
                    v = dot(c, rb[q, HOUT * h : HOUT * h + 256, x : x + 256])
                    pred[out, x : x + 256] += coef[k, out, x : x + 256].astype(F32) * v
        return carry

    lax.fori_loop(0, PAIRS, forward, 0)

    mask = column_of(valid_ref[...].astype(F32))
    for j in range(BLOCKS):
        pred[RIM : RIM + ROWS, 128 * j : 128 * j + 128] *= mask
    res_out = pltpu.make_async_copy(pred.at[pl.ds(RIM, ROWS), :], res_hbm.at[0], sem.at[KERNELS])
    res_out.start()

    acc[...] = jnp.zeros_like(acc)
    low_y = lax.broadcasted_iota(jnp.int32, (ROWS, 128), 1) < 64
    none = jnp.zeros((ROWS, 128), BF16)

    def adjoint(i, carry):
        for q in range(2):
            k = 2 * i + q
            for x in range(0, COLS, 256):
                w[q, 0:EXT, x : x + 256] = (coef[k, :, x : x + 256].astype(F32) * pred[:, x : x + 256]).astype(BF16)
            a = a_ref[k]
            for h in range(2):
                for x in range(0, COLS, 256):
                    cb[q, 128 * h : 128 * h + 128, x : x + 256] = dot(
                        a, w[q, 128 * h : 128 * h + 256, x : x + 256]
                    ).astype(BF16)
        b = b_ref[i]
        for j in range(BLOCKS):
            parts = []
            for q in range(2):
                after = cb[q, :, 128 * j + 128 : 128 * j + 256] if j + 1 < BLOCKS else none
                before = cb[q, :, 128 * j - 128 : 128 * j] if j > 0 else none
                parts += [cb[q, :, 128 * j : 128 * j + 128], jnp.where(low_y, after, before)]
            acc[j] += dot_nt(b, jnp.concatenate(parts, axis=1))
        return carry

    lax.fori_loop(0, PAIRS, adjoint, 0)
    for j in range(BLOCKS):
        send_ref[128 * j : 128 * j + 128, :] = acc[j].astype(BF16)
    res_out.wait()


def main(strip, valid, bands, coefficients, observed, above, below):
    return pl.pallas_call(
        main_kernel,
        out_shape=(
            jax.ShapeDtypeStruct((1, ROWS, COLS), F32),
            jax.ShapeDtypeStruct((COLS, ROWS), BF16),
        ),
        in_specs=[VMEM] * 6 + [ANY] * 4,
        out_specs=(ANY, VMEM),
        scratch_shapes=[
            pltpu.VMEM((BLOCKS, LAT, 128), F32),
            pltpu.VMEM((BLOCKS, LAT, 256), BF16),
            pltpu.VMEM((KERNELS, EXT, COLS), BF16),
            pltpu.VMEM((EXT, COLS), BF16),
            pltpu.VMEM((2, RBR, COLS), BF16),
            pltpu.VMEM((EXT, COLS), F32),
            pltpu.VMEM((2, WR, COLS), BF16),
            pltpu.VMEM((2, ROWS, COLS), BF16),
            pltpu.VMEM((BLOCKS, 128, ROWS), F32),
            pltpu.SemaphoreType.DMA((KERNELS + 5,)),
        ],
        name="main",
    )(strip, valid, *bands, coefficients, observed, above, below)


def gather_kernel(cell_ref, terms_ref, out_ref, total):
    total[...] = jnp.zeros_like(total)
    for e in range(EXPOSURES):
        total[cell_ref[e, 0]] += terms_ref[e].astype(F32)
    for c in range(CELLS):
        out_ref[c] = total[c].T


def gather(cell_of, terms):
    return pl.pallas_call(
        gather_kernel,
        out_shape=jax.ShapeDtypeStruct((CELLS, ROWS, OWN), F32),
        in_specs=[SMEM, VMEM],
        out_specs=VMEM,
        scratch_shapes=[pltpu.VMEM((CELLS, OWN, ROWS), F32)],
        name="gather",
    )(cell_of, terms)


def body(latent, row_taps, column_taps, coefficients, observed, cell_of, valid_rows):
    count = lax.axis_size("row")
    downward = [(i, i + 1) for i in range(count - 1)]
    upward = [(i + 1, i) for i in range(count - 1)]
    sky_above = lax.ppermute(latent[:, ROWS - SKY :], "row", downward)
    sky_below = lax.ppermute(latent[:, :SKY], "row", upward)
    *bands, head, tail = prepare(row_taps, column_taps, valid_rows, observed, coefficients)
    above = lax.ppermute(tail, "row", downward)
    below = lax.ppermute(head, "row", upward)
    packed = pack(cell_of, latent, sky_above, sky_below)
    strip = lax.all_to_all(packed, "exp", 0, 0, tiled=True).reshape(COLS, LATP)
    residual, send = main(strip, valid_rows, bands, coefficients, observed, above, below)
    terms = lax.all_to_all(send.reshape(EXPOSURES, OWN, ROWS), "exp", 0, 0, tiled=True)
    return gather(cell_of, terms), residual


def solution(mesh):
    placed = (
        P(None, "row", "exp"),
        P(),
        P(),
        P("exp", None, "row", None),
        P("exp", "row", None),
        P(),
        P("exp", "row"),
    )
    return jax.shard_map(
        body,
        mesh=mesh,
        in_specs=placed,
        out_specs=(P(None, "row", "exp"), P("exp", "row", None)),
        check_vma=False,
    )
```

```python
import jax
import jax.numpy as jnp
from jax import lax
from jax.experimental import pallas as pl
from jax.experimental.pallas import tpu as pltpu
from jax.sharding import PartitionSpec as P

F32 = jnp.float32
BF16 = jnp.bfloat16
KERNELS = 16
PAIRS = KERNELS // 2
TAPS = 21
HALF = TAPS // 2
CELLS = 4
EXPOSURES = 32
ROWS = 256
COLS = 1024
BLOCKS = COLS // 128
OWN = COLS // EXPOSURES
SKY = 24
RIM = 16
LAT = ROWS + 2 * SKY
LATP = 384
EXT = ROWS + 2 * RIM
HOUT = EXT // 2
TOP = 8
RBR = HOUT + 256
WR = 384

VMEM = pl.BlockSpec(memory_space=pltpu.VMEM)
SMEM = pl.BlockSpec(memory_space=pltpu.SMEM)
ANY = pl.BlockSpec(memory_space=pl.ANY)


def dot(a, b):
    return lax.dot_general(a, b, (((1,), (0,)), ((), ())), preferred_element_type=F32)


def column_of(valid):
    return jnp.broadcast_to(valid, (128, valid.shape[1])).T


def rims_kernel(valid_ref, obs_hbm, coef_hbm, up_ref, down_ref, head, tail, sem):
    copies = [
        pltpu.make_async_copy(coef_hbm.at[0, :, pl.ds(0, RIM), :], head.at[pl.ds(0, KERNELS)], sem.at[0]),
        pltpu.make_async_copy(coef_hbm.at[0, :, pl.ds(ROWS - RIM, RIM), :], tail.at[pl.ds(0, KERNELS)], sem.at[1]),
        pltpu.make_async_copy(obs_hbm.at[0, pl.ds(0, RIM), :], head.at[KERNELS], sem.at[2]),
        pltpu.make_async_copy(obs_hbm.at[0, pl.ds(ROWS - RIM, RIM), :], tail.at[KERNELS], sem.at[3]),
    ]
    for copy in copies:
        copy.start()
    mask = column_of(valid_ref[...].astype(F32))
    head_mask = jnp.concatenate([mask[:RIM]] * BLOCKS, axis=1)
    tail_mask = jnp.concatenate([mask[ROWS - RIM :]] * BLOCKS, axis=1)
    for copy in copies:
        copy.wait()
    for k in range(KERNELS + 1):
        up_ref[k] = (head[k].astype(F32) * head_mask).astype(BF16)
        down_ref[k] = (tail[k].astype(F32) * tail_mask).astype(BF16)


def rims(valid, observed, coefficients):
    rim = (KERNELS + 1, RIM, COLS)
    return pl.pallas_call(
        rims_kernel,
        out_shape=(jax.ShapeDtypeStruct(rim, BF16),) * 2,
        in_specs=[VMEM, ANY, ANY],
        out_specs=(VMEM,) * 2,
        scratch_shapes=[pltpu.VMEM(rim, BF16), pltpu.VMEM(rim, BF16), pltpu.SemaphoreType.DMA((4,))],
        name="rims",
    )(valid, observed, coefficients)


def base_rows(taps, place):
    lane = lax.broadcasted_iota(jnp.int32, (KERNELS, 256), 1)
    out = jnp.zeros((KERNELS, 256), F32)
    for t in range(TAPS):
        out = jnp.where(lane == place(t) % 256, taps[:, t : t + 1], out)
    return out


def skewed(row, count):
    return pltpu.roll(jnp.broadcast_to(row, (count, 256)), 0, 1, stride=1, stride_axis=0)


def bands_kernel(row_ref, col_ref, f_ref, c_ref, a_ref, b_ref):
    rows = row_ref[...].astype(F32)
    cols = col_ref[...].astype(F32)
    f_base = base_rows(rows, lambda t: HALF - t)
    b_base = base_rows(rows, lambda t: t - HALF)
    c_base = base_rows(cols, lambda t: t + 2 * RIM - RIM - HALF)
    a_base = base_rows(cols, lambda t: RIM + HALF - t)
    at = lax.broadcasted_iota(jnp.int32, (256, 256), 0)
    out = lax.broadcasted_iota(jnp.int32, (256, 256), 1)
    near = jnp.abs(at - out) < 128
    for k in range(KERNELS):
        i, q = k // 2, k % 2
        f_ref[i, :, 128 * q : 128 * q + 128] = skewed(f_base[k : k + 1], 256)[:, :128].astype(BF16)
        b = skewed(b_base[k : k + 1], 256)
        b_ref[i, 256 * q : 256 * q + 256, :] = jnp.where(near, b, 0.0).astype(BF16)
        far = jnp.where(near, 0.0, b).astype(BF16)
        b_ref[i, 512 + 128 * q : 576 + 128 * q, :] = far[:64]
        b_ref[i, 576 + 128 * q : 640 + 128 * q, :] = far[192:]
        c_ref[k] = skewed(c_base[k : k + 1], HOUT).astype(BF16)
        a_ref[k] = skewed(a_base[k : k + 1], 128).astype(BF16)


def make_bands(row_taps, column_taps):
    return pl.pallas_call(
        bands_kernel,
        out_shape=(
            jax.ShapeDtypeStruct((PAIRS, 256, 256), BF16),
            jax.ShapeDtypeStruct((KERNELS, HOUT, 256), BF16),
            jax.ShapeDtypeStruct((KERNELS, 128, 256), BF16),
            jax.ShapeDtypeStruct((PAIRS, 768, 256), BF16),
        ),
        in_specs=[VMEM, VMEM],
        out_specs=(VMEM,) * 4,
        name="bands",
    )(row_taps, column_taps)


def pack_kernel(cell_ref, lat_ref, above_ref, below_ref, after_ref, out_ref, turned):
    for c in range(CELLS):
        turned[c] = jnp.concatenate(
            [above_ref[c], lat_ref[c], below_ref[c], jnp.zeros((OWN, LATP - LAT), BF16)], axis=1
        )
    for e in range(EXPOSURES):
        out_ref[e] = turned[cell_ref[0, e]]


def pack(cell_of, latent, above, below, after):
    return pl.pallas_call(
        pack_kernel,
        out_shape=jax.ShapeDtypeStruct((EXPOSURES, OWN, LATP), BF16),
        in_specs=[SMEM, VMEM, VMEM, VMEM, ANY],
        out_specs=VMEM,
        scratch_shapes=[pltpu.VMEM((CELLS, OWN, LATP), BF16)],
        name="pack",
    )(cell_of, latent, above, below, after)


def main_kernel(
    strip_hbm, valid_ref, f_hbm, c_hbm, a_hbm, b_hbm, coef_hbm, obs_hbm, above_hbm, below_hbm,
    res_hbm, send_ref,
    strip_ref, f_ref, c_ref, a_ref, b_ref, sky, windows, coef, obs, rb, rb2, pred, w, w2, cb, cb2, acc, sem, rim_sem, band_sem,
):
    def coef_in(k):
        return pltpu.make_async_copy(coef_hbm.at[0, k], coef.at[k, pl.ds(RIM, ROWS), :], sem.at[k])

    pairs = ((f_hbm, f_ref), (c_hbm, c_ref), (a_hbm, a_ref), (b_hbm, b_ref), (strip_hbm, strip_ref))
    f_in, c_in, a_in, b_in, strip_in = (
        pltpu.make_async_copy(s, d, band_sem.at[n]) for n, (s, d) in enumerate(pairs)
    )
    rims_in = [
        pltpu.make_async_copy(obs_hbm.at[0], obs.at[pl.ds(RIM, ROWS), :], rim_sem.at[0]),
        pltpu.make_async_copy(above_hbm.at[KERNELS], obs.at[pl.ds(0, RIM), :], rim_sem.at[1]),
        pltpu.make_async_copy(below_hbm.at[KERNELS], obs.at[pl.ds(RIM + ROWS, RIM), :], rim_sem.at[2]),
        pltpu.make_async_copy(above_hbm.at[pl.ds(0, KERNELS)], coef.at[:, pl.ds(0, RIM), :], rim_sem.at[3]),
        pltpu.make_async_copy(
            below_hbm.at[pl.ds(0, KERNELS)], coef.at[:, pl.ds(RIM + ROWS, RIM), :], rim_sem.at[4]
        ),
    ]
    strip_in.start()
    for copy in rims_in[:3]:
        copy.start()
    f_in.start()
    for copy in rims_in[3:]:
        copy.start()
    c_in.start()
    for k in range(KERNELS):
        coef_in(k).start()
    a_in.start()
    b_in.start()

    for r in (rb, rb2):
        r[:, :, 0:TOP, :] = jnp.zeros((2, BLOCKS, TOP, 128), BF16)
        r[:, :, TOP + LAT :, :] = jnp.zeros((2, BLOCKS, RBR - LAT - TOP, 128), BF16)
    for r in (w, w2):
        r[:, :, EXT:, :] = jnp.zeros((2, BLOCKS, WR - EXT, 128), BF16)
    acc[...] = jnp.zeros_like(acc)
    low = lax.broadcasted_iota(jnp.int32, (LAT, 128), 1) < 64
    strip_in.wait()
    for j in range(BLOCKS):
        sky[j] = strip_ref[128 * j : 128 * j + 128, :].astype(F32).T[:LAT]
    zero = jnp.zeros((LAT, 128), F32)
    for j in range(BLOCKS):
        after = sky[j + 1] if j + 1 < BLOCKS else zero
        before = sky[j - 1] if j > 0 else zero
        windows[j, :, 0:128] = sky[j].astype(BF16)
        windows[j, :, 128:256] = jnp.where(low, after, before).astype(BF16)
    for copy in rims_in[:3]:
        copy.wait()
    pred[...] = -obs[...].astype(F32)
    f_in.wait()
    for copy in rims_in[3:]:
        copy.wait()
    c_in.wait()

    def blur(i, rb):
        f = f_ref[i]
        for j in range(BLOCKS):
            both = dot(windows[j], f)
            rb[0, j, TOP : TOP + LAT, :] = both[:, :128].astype(BF16)
            rb[1, j, TOP : TOP + LAT, :] = both[:, 128:].astype(BF16)

    def predict(i, rb):
        for q in range(2):
            k = 2 * i + q
            c = c_ref[k]
            for h in range(2):
                out = slice(HOUT * h, HOUT * h + HOUT)
                for x in range(0, BLOCKS, 2):
                    at = slice(HOUT * h, HOUT * h + 256)
                    v = dot(c, jnp.concatenate([rb[q, x, at, :], rb[q, x + 1, at, :]], axis=1))
                    cols = slice(128 * x, 128 * x + 256)
                    pred[out, cols] += coef[k, out, cols].astype(F32) * v

    def forward(n, carry):
        for m in range(4):
            coef_in(4 * n + m).wait()
        blur(2 * n, rb)
        blur(2 * n + 1, rb2)
        predict(2 * n, rb)
        predict(2 * n + 1, rb2)
        return carry

    lax.fori_loop(0, PAIRS // 2, forward, 0)

    mask = column_of(valid_ref[...].astype(F32))
    for j in range(BLOCKS):
        pred[RIM : RIM + ROWS, 128 * j : 128 * j + 128] *= mask
    res_out = pltpu.make_async_copy(pred.at[pl.ds(RIM, ROWS), :], res_hbm.at[0], rim_sem.at[0])
    res_out.start()

    low_y = lax.broadcasted_iota(jnp.int32, (ROWS, 128), 1) < 64
    none = jnp.zeros((ROWS, 128), BF16)
    a_in.wait()
    b_in.wait()

    def weigh(i, w):
        for q in range(2):
            for x in range(BLOCKS):
                cols = slice(128 * x, 128 * x + 128)
                w[q, x, 0:EXT, :] = (coef[2 * i + q, :, cols].astype(F32) * pred[:, cols]).astype(BF16)

    def back(i, w, cb):
        for q in range(2):
            a = a_ref[2 * i + q]
            for h in range(2):
                for x in range(0, BLOCKS, 2):
                    at = slice(128 * h, 128 * h + 256)
                    both = dot(a, jnp.concatenate([w[q, x, at, :], w[q, x + 1, at, :]], axis=1))
                    cb[q, x, 128 * h : 128 * h + 128, :] = both[:, :128].astype(BF16)
                    cb[q, x + 1, 128 * h : 128 * h + 128, :] = both[:, 128:].astype(BF16)
        b = b_ref[i]
        for x in range(0, BLOCKS, 2):
            parts = [cb[0, x], cb[0, x + 1], cb[1, x], cb[1, x + 1]]
            for q in range(2):
                after = cb[q, x + 2] if x + 2 < BLOCKS else none
                before = cb[q, x - 1] if x > 0 else none
                parts.append(jnp.where(low_y, after, before))
            acc[x // 2] += dot(jnp.concatenate(parts, axis=1), b)

    weigh(0, w)

    def adjoint(n, carry):
        weigh(2 * n + 1, w2)
        back(2 * n, w, cb)
        weigh(jnp.minimum(2 * n + 2, PAIRS - 1), w)
        back(2 * n + 1, w2, cb2)
        return carry

    lax.fori_loop(0, PAIRS // 2, adjoint, 0)
    for x in range(BLOCKS // 2):
        send_ref[256 * x : 256 * x + 256, :] = acc[x].T.astype(BF16)
    res_out.wait()


def main(strip, valid, bands, coefficients, observed, above, below):
    return pl.pallas_call(
        main_kernel,
        out_shape=(
            jax.ShapeDtypeStruct((1, ROWS, COLS), F32),
            jax.ShapeDtypeStruct((COLS, ROWS), BF16),
        ),
        in_specs=[ANY, VMEM] + [ANY] * 8,
        out_specs=(ANY, VMEM),
        scratch_shapes=[
            pltpu.VMEM((COLS, LATP), BF16),
            pltpu.VMEM((PAIRS, 256, 256), BF16),
            pltpu.VMEM((KERNELS, HOUT, 256), BF16),
            pltpu.VMEM((KERNELS, 128, 256), BF16),
            pltpu.VMEM((PAIRS, 768, 256), BF16),
            pltpu.VMEM((BLOCKS, LAT, 128), F32),
            pltpu.VMEM((BLOCKS, LAT, 256), BF16),
            pltpu.VMEM((KERNELS, EXT, COLS), BF16),
            pltpu.VMEM((EXT, COLS), BF16),
            pltpu.VMEM((2, BLOCKS, RBR, 128), BF16),
            pltpu.VMEM((2, BLOCKS, RBR, 128), BF16),
            pltpu.VMEM((EXT, COLS), F32),
            pltpu.VMEM((2, BLOCKS, WR, 128), BF16),
            pltpu.VMEM((2, BLOCKS, WR, 128), BF16),
            pltpu.VMEM((2, BLOCKS, ROWS, 128), BF16),
            pltpu.VMEM((2, BLOCKS, ROWS, 128), BF16),
            pltpu.VMEM((BLOCKS // 2, ROWS, 256), F32),
            pltpu.SemaphoreType.DMA((KERNELS,)),
            pltpu.SemaphoreType.DMA((5,)),
            pltpu.SemaphoreType.DMA((5,)),
        ],
        name="main",
    )(strip, valid, *bands, coefficients, observed, above, below)


def gather_kernel(cell_ref, terms_ref, out_ref):
    out_ref[...] = jnp.zeros_like(out_ref)
    for e in range(EXPOSURES):
        out_ref[cell_ref[0, e]] += terms_ref[e].astype(F32)


def gather(cell_of, terms):
    return pl.pallas_call(
        gather_kernel,
        out_shape=jax.ShapeDtypeStruct((CELLS, OWN, ROWS), F32),
        in_specs=[SMEM, VMEM],
        out_specs=VMEM,
        name="gather",
    )(cell_of, terms)


def body(latent, row_taps, column_taps, coefficients, observed, cell_of, valid_rows):
    count = lax.axis_size("row")
    downward = [(i, i + 1) for i in range(count - 1)]
    upward = [(i + 1, i) for i in range(count - 1)]
    cell_of = cell_of.reshape(1, EXPOSURES)
    latent = jnp.swapaxes(latent, 1, 2)
    sky_above = lax.ppermute(latent[:, :, ROWS - SKY :], "row", downward)
    sky_below = lax.ppermute(latent[:, :, :SKY], "row", upward)
    head, tail = rims(valid_rows, observed, coefficients)
    above = lax.ppermute(tail, "row", downward)
    below = lax.ppermute(head, "row", upward)
    packed = pack(cell_of, latent, sky_above, sky_below, head)
    bands = make_bands(row_taps, column_taps)
    strip = lax.all_to_all(packed, "exp", 0, 0, tiled=True).reshape(COLS, LATP)
    residual, send = main(strip, valid_rows, bands, coefficients, observed, above, below)
    terms = lax.all_to_all(send.reshape(EXPOSURES, OWN, ROWS), "exp", 0, 0, tiled=True)
    return jnp.swapaxes(gather(cell_of, terms), 1, 2), residual


def solution(mesh):
    placed = (
        P(None, "row", "exp"),
        P(),
        P(),
        P("exp", None, "row", None),
        P("exp", "row", None),
        P(),
        P("exp", "row"),
    )
    return jax.shard_map(
        body,
        mesh=mesh,
        in_specs=placed,
        out_specs=(P(None, "row", "exp"), P("exp", "row", None)),
        check_vma=False,
    )
```

```python
import jax
import jax.numpy as jnp
from jax import lax
from jax.experimental import pallas as pl
from jax.experimental.pallas import tpu as pltpu
from jax.sharding import PartitionSpec as P


F32 = jnp.float32
BF16 = jnp.bfloat16
KERNELS = 16
PAIRS = KERNELS // 2
TAPS = 21
HALF = TAPS // 2
CELLS = 4
EXPOSURES = 32
ROWS = 256
COLS = 1024
BLOCKS = COLS // 128
OWN = COLS // EXPOSURES
SKY = 24
RIM = 16
LAT = ROWS + 2 * SKY
LATP = 384
EXT = ROWS + 2 * RIM
HOUT = EXT // 2
TOP = 8
RBR = HOUT + 256
WR = 384

VMEM = pl.BlockSpec(memory_space=pltpu.VMEM)
SMEM = pl.BlockSpec(memory_space=pltpu.SMEM)
ANY = pl.BlockSpec(memory_space=pl.ANY)


def dot(a, b):
    return lax.dot_general(a, b, (((1,), (0,)), ((), ())), preferred_element_type=F32)


def column_of(valid):
    return jnp.broadcast_to(valid, (128, valid.shape[1])).T


def stage_kernel(
    cell_ref, lat_ref, above_ref, below_ref, valid_ref, obs_hbm, coef_hbm,
    packed_hbm, up_hbm, down_hbm,
    turned, packed, head, tail, sem, out_sem,
):
    last = pl.ds(ROWS - RIM, RIM)
    copies = [
        pltpu.make_async_copy(coef_hbm.at[0, :, pl.ds(0, RIM), :], head.at[pl.ds(0, KERNELS)], sem.at[0]),
        pltpu.make_async_copy(coef_hbm.at[0, :, last, :], tail.at[pl.ds(0, KERNELS)], sem.at[1]),
        pltpu.make_async_copy(obs_hbm.at[0, pl.ds(0, RIM), :], head.at[KERNELS], sem.at[2]),
        pltpu.make_async_copy(obs_hbm.at[0, last, :], tail.at[KERNELS], sem.at[3]),
    ]
    outs = [
        pltpu.make_async_copy(packed, packed_hbm, out_sem.at[0]),
        pltpu.make_async_copy(head, up_hbm, out_sem.at[1]),
        pltpu.make_async_copy(tail, down_hbm, out_sem.at[2]),
    ]
    for copy in copies:
        copy.start()
    fill = jnp.zeros((OWN, LATP - LAT), BF16)
    for c in range(CELLS):
        parts = [above_ref[c][:, ROWS - SKY :], lat_ref[c], below_ref[c][:, :SKY], fill]
        turned[c] = jnp.concatenate(parts, axis=1)
    for e in range(EXPOSURES):
        packed[e] = turned[cell_ref[0, e]]
    outs[0].start()
    mask = column_of(valid_ref[...].astype(F32))
    head_mask = jnp.concatenate([mask[:RIM]] * BLOCKS, axis=1)
    tail_mask = jnp.concatenate([mask[ROWS - RIM :]] * BLOCKS, axis=1)
    for copy in copies:
        copy.wait()
    for k in range(KERNELS + 1):
        head[k] = (head[k].astype(F32) * head_mask).astype(BF16)
    outs[1].start()
    for k in range(KERNELS + 1):
        tail[k] = (tail[k].astype(F32) * tail_mask).astype(BF16)
    outs[2].start()
    for copy in outs:
        copy.wait()


def stage(cell_of, latent, above, below, valid, observed, coefficients):
    rim = (KERNELS + 1, RIM, COLS)
    packed = (EXPOSURES, OWN, LATP)
    return pl.pallas_call(
        stage_kernel,
        out_shape=(jax.ShapeDtypeStruct(packed, BF16),) + (jax.ShapeDtypeStruct(rim, BF16),) * 2,
        in_specs=[SMEM, VMEM, VMEM, VMEM, VMEM, ANY, ANY],
        out_specs=(ANY,) * 3,
        scratch_shapes=[
            pltpu.VMEM((CELLS, OWN, LATP), BF16),
            pltpu.VMEM(packed, BF16),
            pltpu.VMEM(rim, BF16),
            pltpu.VMEM(rim, BF16),
            pltpu.SemaphoreType.DMA((4,)),
            pltpu.SemaphoreType.DMA((3,)),
        ],
        name="stage",
    )(cell_of, latent, above, below, valid, observed, coefficients)


def base_rows(taps, place):
    lane = lax.broadcasted_iota(jnp.int32, (KERNELS, 256), 1)
    out = jnp.zeros((KERNELS, 256), F32)
    for t in range(TAPS):
        out = jnp.where(lane == place(t) % 256, taps[:, t : t + 1], out)
    return out


def skewed(row, count):
    return pltpu.roll(jnp.broadcast_to(row, (count, 256)), 0, 1, stride=1, stride_axis=0)


def bands_kernel(row_ref, col_ref, f_ref, c_ref, a_ref, b_ref):
    rows = row_ref[...].astype(F32)
    cols = col_ref[...].astype(F32)
    f_base = base_rows(rows, lambda t: HALF - t)
    b_base = base_rows(rows, lambda t: t - HALF)
    c_base = base_rows(cols, lambda t: t + 2 * RIM - RIM - HALF)
    a_base = base_rows(cols, lambda t: RIM + HALF - t)
    at = lax.broadcasted_iota(jnp.int32, (256, 256), 0)
    out = lax.broadcasted_iota(jnp.int32, (256, 256), 1)
    near = jnp.abs(at - out) < 128
    for k in range(KERNELS):
        i, q = k // 2, k % 2
        f_ref[i, :, 128 * q : 128 * q + 128] = skewed(f_base[k : k + 1], 256)[:, :128].astype(BF16)
        b = skewed(b_base[k : k + 1], 256)
        b_ref[i, 256 * q : 256 * q + 256, :] = jnp.where(near, b, 0.0).astype(BF16)
        far = jnp.where(near, 0.0, b).astype(BF16)
        b_ref[i, 512 + 128 * q : 576 + 128 * q, :] = far[:64]
        b_ref[i, 576 + 128 * q : 640 + 128 * q, :] = far[192:]
        c_ref[k] = skewed(c_base[k : k + 1], HOUT).astype(BF16)
        a_ref[k] = skewed(a_base[k : k + 1], 128).astype(BF16)


def make_bands(row_taps, column_taps):
    return pl.pallas_call(
        bands_kernel,
        out_shape=(
            jax.ShapeDtypeStruct((PAIRS, 256, 256), BF16),
            jax.ShapeDtypeStruct((KERNELS, HOUT, 256), BF16),
            jax.ShapeDtypeStruct((KERNELS, 128, 256), BF16),
            jax.ShapeDtypeStruct((PAIRS, 768, 256), BF16),
        ),
        in_specs=[VMEM, VMEM],
        out_specs=(VMEM,) * 4,
        name="bands",
    )(row_taps, column_taps)


def main_kernel(
    strip_hbm, valid_ref, f_hbm, c_hbm, a_hbm, b_hbm, coef_hbm, obs_hbm, above_hbm, below_hbm,
    res_hbm, send_ref,
    strip_ref, f_ref, c_ref, a_ref, b_ref, sky, windows, coef, obs, rb, rb2, pred, w, w2, cb, cb2, acc, sem, rim_sem, band_sem,
):
    def coef_in(k):
        return pltpu.make_async_copy(coef_hbm.at[0, k], coef.at[k, pl.ds(RIM, ROWS), :], sem.at[k])

    pairs = ((f_hbm, f_ref), (c_hbm, c_ref), (a_hbm, a_ref), (b_hbm, b_ref), (strip_hbm, strip_ref))
    f_in, c_in, a_in, b_in, strip_in = (
        pltpu.make_async_copy(s, d, band_sem.at[n]) for n, (s, d) in enumerate(pairs)
    )
    rims_in = [
        pltpu.make_async_copy(obs_hbm.at[0], obs.at[pl.ds(RIM, ROWS), :], rim_sem.at[0]),
        pltpu.make_async_copy(above_hbm.at[KERNELS], obs.at[pl.ds(0, RIM), :], rim_sem.at[1]),
        pltpu.make_async_copy(below_hbm.at[KERNELS], obs.at[pl.ds(RIM + ROWS, RIM), :], rim_sem.at[2]),
        pltpu.make_async_copy(above_hbm.at[pl.ds(0, KERNELS)], coef.at[:, pl.ds(0, RIM), :], rim_sem.at[3]),
        pltpu.make_async_copy(
            below_hbm.at[pl.ds(0, KERNELS)], coef.at[:, pl.ds(RIM + ROWS, RIM), :], rim_sem.at[4]
        ),
    ]
    strip_in.start()
    for copy in rims_in[:3]:
        copy.start()
    f_in.start()
    for copy in rims_in[3:]:
        copy.start()
    c_in.start()
    for k in range(KERNELS):
        coef_in(k).start()
    a_in.start()
    b_in.start()

    for r in (rb, rb2):
        r[:, :, 0:TOP, :] = jnp.zeros((2, BLOCKS, TOP, 128), BF16)
        r[:, :, TOP + LAT :, :] = jnp.zeros((2, BLOCKS, RBR - LAT - TOP, 128), BF16)
    for r in (w, w2):
        r[:, :, EXT:, :] = jnp.zeros((2, BLOCKS, WR - EXT, 128), BF16)
    acc[...] = jnp.zeros_like(acc)
    low = lax.broadcasted_iota(jnp.int32, (LAT, 128), 1) < 64
    strip_in.wait()
    for j in range(BLOCKS):
        sky[j] = strip_ref[128 * j : 128 * j + 128, :].astype(F32).T[:LAT]
    zero = jnp.zeros((LAT, 128), F32)
    for j in range(BLOCKS):
        after = sky[j + 1] if j + 1 < BLOCKS else zero
        before = sky[j - 1] if j > 0 else zero
        windows[j, :, 0:128] = sky[j].astype(BF16)
        windows[j, :, 128:256] = jnp.where(low, after, before).astype(BF16)
    for copy in rims_in[:3]:
        copy.wait()
    pred[...] = -obs[...].astype(F32)
    f_in.wait()
    for copy in rims_in[3:]:
        copy.wait()
    c_in.wait()

    def blur(i, rb):
        f = f_ref[i]
        for j in range(BLOCKS):
            both = dot(windows[j], f)
            rb[0, j, TOP : TOP + LAT, :] = both[:, :128].astype(BF16)
            rb[1, j, TOP : TOP + LAT, :] = both[:, 128:].astype(BF16)

    def predict(i, rb):
        for q in range(2):
            k = 2 * i + q
            c = c_ref[k]
            for h in range(2):
                out = slice(HOUT * h, HOUT * h + HOUT)
                for x in range(0, BLOCKS, 2):
                    at = slice(HOUT * h, HOUT * h + 256)
                    v = dot(c, jnp.concatenate([rb[q, x, at, :], rb[q, x + 1, at, :]], axis=1))
                    cols = slice(128 * x, 128 * x + 256)
                    pred[out, cols] += coef[k, out, cols].astype(F32) * v

    def forward(n, carry):
        for m in range(4):
            coef_in(4 * n + m).wait()
        blur(2 * n, rb)
        blur(2 * n + 1, rb2)
        predict(2 * n, rb)
        predict(2 * n + 1, rb2)
        return carry

    lax.fori_loop(0, PAIRS // 2, forward, 0)

    mask = column_of(valid_ref[...].astype(F32))
    for j in range(BLOCKS):
        pred[RIM : RIM + ROWS, 128 * j : 128 * j + 128] *= mask
    res_out = pltpu.make_async_copy(pred.at[pl.ds(RIM, ROWS), :], res_hbm.at[0], rim_sem.at[0])
    res_out.start()

    low_y = lax.broadcasted_iota(jnp.int32, (ROWS, 128), 1) < 64
    none = jnp.zeros((ROWS, 128), BF16)
    a_in.wait()
    b_in.wait()

    def weigh(i, w):
        for q in range(2):
            for x in range(BLOCKS):
                cols = slice(128 * x, 128 * x + 128)
                w[q, x, 0:EXT, :] = (coef[2 * i + q, :, cols].astype(F32) * pred[:, cols]).astype(BF16)

    def back(i, w, cb):
        for q in range(2):
            a = a_ref[2 * i + q]
            for h in range(2):
                for x in range(0, BLOCKS, 2):
                    at = slice(128 * h, 128 * h + 256)
                    both = dot(a, jnp.concatenate([w[q, x, at, :], w[q, x + 1, at, :]], axis=1))
                    cb[q, x, 128 * h : 128 * h + 128, :] = both[:, :128].astype(BF16)
                    cb[q, x + 1, 128 * h : 128 * h + 128, :] = both[:, 128:].astype(BF16)
        b = b_ref[i]
        for x in range(0, BLOCKS, 2):
            parts = [cb[0, x], cb[0, x + 1], cb[1, x], cb[1, x + 1]]
            for q in range(2):
                after = cb[q, x + 2] if x + 2 < BLOCKS else none
                before = cb[q, x - 1] if x > 0 else none
                parts.append(jnp.where(low_y, after, before))
            acc[x // 2] += dot(jnp.concatenate(parts, axis=1), b)

    weigh(0, w)

    def adjoint(n, carry):
        weigh(2 * n + 1, w2)
        back(2 * n, w, cb)
        weigh(jnp.minimum(2 * n + 2, PAIRS - 1), w)
        back(2 * n + 1, w2, cb2)
        return carry

    lax.fori_loop(0, PAIRS // 2, adjoint, 0)
    for x in range(BLOCKS // 2):
        send_ref[256 * x : 256 * x + 256, :] = acc[x].T.astype(BF16)
    res_out.wait()


def main(strip, valid, bands, coefficients, observed, above, below):
    return pl.pallas_call(
        main_kernel,
        out_shape=(
            jax.ShapeDtypeStruct((1, ROWS, COLS), F32),
            jax.ShapeDtypeStruct((COLS, ROWS), BF16),
        ),
        in_specs=[ANY, VMEM] + [ANY] * 8,
        out_specs=(ANY, VMEM),
        scratch_shapes=[
            pltpu.VMEM((COLS, LATP), BF16),
            pltpu.VMEM((PAIRS, 256, 256), BF16),
            pltpu.VMEM((KERNELS, HOUT, 256), BF16),
            pltpu.VMEM((KERNELS, 128, 256), BF16),
            pltpu.VMEM((PAIRS, 768, 256), BF16),
            pltpu.VMEM((BLOCKS, LAT, 128), F32),
            pltpu.VMEM((BLOCKS, LAT, 256), BF16),
            pltpu.VMEM((KERNELS, EXT, COLS), BF16),
            pltpu.VMEM((EXT, COLS), BF16),
            pltpu.VMEM((2, BLOCKS, RBR, 128), BF16),
            pltpu.VMEM((2, BLOCKS, RBR, 128), BF16),
            pltpu.VMEM((EXT, COLS), F32),
            pltpu.VMEM((2, BLOCKS, WR, 128), BF16),
            pltpu.VMEM((2, BLOCKS, WR, 128), BF16),
            pltpu.VMEM((2, BLOCKS, ROWS, 128), BF16),
            pltpu.VMEM((2, BLOCKS, ROWS, 128), BF16),
            pltpu.VMEM((BLOCKS // 2, ROWS, 256), F32),
            pltpu.SemaphoreType.DMA((KERNELS,)),
            pltpu.SemaphoreType.DMA((5,)),
            pltpu.SemaphoreType.DMA((5,)),
        ],
        name="main",
    )(strip, valid, *bands, coefficients, observed, above, below)


def gather_kernel(cell_ref, terms_ref, out_ref):
    out_ref[...] = jnp.zeros_like(out_ref)
    for e in range(EXPOSURES):
        out_ref[cell_ref[0, e]] += terms_ref[e].astype(F32)


def gather(cell_of, terms):
    return pl.pallas_call(
        gather_kernel,
        out_shape=jax.ShapeDtypeStruct((CELLS, OWN, ROWS), F32),
        in_specs=[SMEM, VMEM],
        out_specs=VMEM,
        name="gather",
    )(cell_of, terms)


def body(latent, row_taps, column_taps, coefficients, observed, cell_of, valid_rows):
    count = lax.axis_size("row")
    downward = [(i, i + 1) for i in range(count - 1)]
    upward = [(i + 1, i) for i in range(count - 1)]
    cell_of = cell_of.reshape(1, EXPOSURES)
    latent = jnp.swapaxes(latent, 1, 2)
    sky_above = lax.ppermute(latent, "row", downward)
    sky_below = lax.ppermute(latent, "row", upward)
    packed, head, tail = stage(cell_of, latent, sky_above, sky_below, valid_rows, observed, coefficients)
    above = lax.ppermute(tail, "row", downward)
    below = lax.ppermute(head, "row", upward)
    strip = lax.all_to_all(packed, "exp", 0, 0, tiled=True)
    bands = make_bands(row_taps, column_taps)
    strip = strip.reshape(COLS, LATP)
    residual, send = main(strip, valid_rows, bands, coefficients, observed, above, below)
    terms = lax.all_to_all(send.reshape(EXPOSURES, OWN, ROWS), "exp", 0, 0, tiled=True)
    return jnp.swapaxes(gather(cell_of, terms), 1, 2), residual


def solution(mesh):
    placed = (
        P(None, "row", "exp"),
        P(),
        P(),
        P("exp", None, "row", None),
        P("exp", "row", None),
        P(),
        P("exp", "row"),
    )
    return jax.shard_map(
        body,
        mesh=mesh,
        in_specs=placed,
        out_specs=(P(None, "row", "exp"), P("exp", "row", None)),
        check_vma=False,
    )
```

```python
import jax
import jax.numpy as jnp
from jax import lax
from jax.experimental import pallas as pl
from jax.experimental.pallas import tpu as pltpu
from jax.sharding import PartitionSpec as P


F32 = jnp.float32
BF16 = jnp.bfloat16
KERNELS = 16
PAIRS = KERNELS // 2
TAPS = 21
HALF = TAPS // 2
CELLS = 4
EXPOSURES = 32
ROWS = 256
COLS = 1024
BLOCKS = COLS // 128
OWN = COLS // EXPOSURES
SKY = 24
RIM = 16
LAT = ROWS + 2 * SKY
LATP = 384
EXT = ROWS + 2 * RIM
HOUT = EXT // 2
TOP = 8
RBR = HOUT + 256
WR = 384

VMEM = pl.BlockSpec(memory_space=pltpu.VMEM)
SMEM = pl.BlockSpec(memory_space=pltpu.SMEM)
ANY = pl.BlockSpec(memory_space=pl.ANY)
HBM = pl.BlockSpec(memory_space=pltpu.HBM)


def dot(a, b):
    return lax.dot_general(a, b, (((1,), (0,)), ((), ())), preferred_element_type=F32)


def column_of(valid):
    return jnp.broadcast_to(valid, (128, valid.shape[1])).T


def pack_kernel(even_ref, cell_ref, lat_ref, near_ref, far_ref, out_ref, turned):
    even = even_ref[0, 0] > 0
    fill = jnp.zeros((OWN, LATP - LAT), F32)
    for c in range(CELLS):
        near, far = near_ref[c].astype(F32), far_ref[c].astype(F32)
        above = jnp.where(even, far[:, ROWS - SKY :], near[:, ROWS - SKY :])
        below = jnp.where(even, near[:, :SKY], far[:, :SKY])
        turned[c] = jnp.concatenate([above, lat_ref[c].astype(F32), below, fill], axis=1).astype(BF16)
    for e in range(EXPOSURES):
        out_ref[e] = turned[cell_ref[0, e]]


def pack(even, cell_of, latent, near, far):
    return pl.pallas_call(
        pack_kernel,
        out_shape=jax.ShapeDtypeStruct((EXPOSURES, OWN, LATP), BF16),
        in_specs=[SMEM, SMEM, VMEM, VMEM, VMEM],
        out_specs=VMEM,
        scratch_shapes=[pltpu.VMEM((CELLS, OWN, LATP), BF16)],
        name="pack",
    )(even, cell_of, latent, near, far)


def base_rows(taps, place):
    lane = lax.broadcasted_iota(jnp.int32, (KERNELS, 256), 1)
    out = jnp.zeros((KERNELS, 256), F32)
    for t in range(TAPS):
        out = jnp.where(lane == place(t) % 256, taps[:, t : t + 1], out)
    return out


def skewed(row, count):
    return pltpu.roll(jnp.broadcast_to(row, (count, 256)), 0, 1, stride=1, stride_axis=0)


def bands_kernel(row_ref, col_ref, f_ref, c_hbm, a_hbm, b_hbm, c_ref, a_ref, b_ref, sem):
    c_out = pltpu.make_async_copy(c_ref, c_hbm, sem.at[PAIRS + 1])
    a_out = pltpu.make_async_copy(a_ref, a_hbm, sem.at[PAIRS])
    b_out = [pltpu.make_async_copy(b_ref.at[i], b_hbm.at[i], sem.at[i]) for i in range(PAIRS)]
    rows = row_ref[...].astype(F32)
    cols = col_ref[...].astype(F32)
    f_base = base_rows(rows, lambda t: HALF - t)
    b_base = base_rows(rows, lambda t: t - HALF)
    c_base = base_rows(cols, lambda t: t + 2 * RIM - RIM - HALF)
    a_base = base_rows(cols, lambda t: RIM + HALF - t)
    at = lax.broadcasted_iota(jnp.int32, (256, 256), 0)
    out = lax.broadcasted_iota(jnp.int32, (256, 256), 1)
    near = jnp.abs(at - out) < 128
    for k in range(KERNELS):
        i, q = k // 2, k % 2
        f_ref[i, :, 128 * q : 128 * q + 128] = skewed(f_base[k : k + 1], 256)[:, :128].astype(BF16)
        b = skewed(b_base[k : k + 1], 256)
        b_ref[i, 256 * q : 256 * q + 256, :] = jnp.where(near, b, 0.0).astype(BF16)
        far = jnp.where(near, 0.0, b).astype(BF16)
        b_ref[i, 512 + 128 * q : 576 + 128 * q, :] = far[:64]
        b_ref[i, 576 + 128 * q : 640 + 128 * q, :] = far[192:]
        c_ref[k] = skewed(c_base[k : k + 1], HOUT).astype(BF16)
        a_ref[k] = skewed(a_base[k : k + 1], 128).astype(BF16)
        if q == 1:
            b_out[i].start()
    c_out.start()
    a_out.start()
    for copy in (*b_out, c_out, a_out):
        copy.wait()


def make_bands(row_taps, column_taps):
    return pl.pallas_call(
        bands_kernel,
        out_shape=(
            jax.ShapeDtypeStruct((PAIRS, 256, 256), BF16),
            jax.ShapeDtypeStruct((KERNELS, HOUT, 256), BF16),
            jax.ShapeDtypeStruct((KERNELS, 128, 256), BF16),
            jax.ShapeDtypeStruct((PAIRS, 768, 256), BF16),
        ),
        in_specs=[VMEM, VMEM],
        out_specs=(VMEM, HBM, HBM, HBM),
        scratch_shapes=[
            pltpu.VMEM((KERNELS, HOUT, 256), BF16),
            pltpu.VMEM((KERNELS, 128, 256), BF16),
            pltpu.VMEM((PAIRS, 768, 256), BF16),
            pltpu.SemaphoreType.DMA((PAIRS + 2,)),
        ],
        compiler_params=pltpu.CompilerParams(vmem_limit_bytes=56 << 20),
        name="bands",
    )(row_taps, column_taps)


def main_kernel(
    even_ref, strip_ref, valid_ref, f_hbm, c_hbm, a_hbm, b_hbm, coef_hbm, obs_hbm, near_hbm, far_hbm,
    res_hbm, send_ref,
    f_ref, c_ref, a_ref, b_ref, sky, windows, coef, obs, rb, rb2, pred, w, w2, cb, cb2, acc, sem, rim_sem, band_sem,
):
    def coef_in(k):
        return pltpu.make_async_copy(coef_hbm.at[0, k], coef.at[k, pl.ds(RIM, ROWS), :], sem.at[k])

    even = even_ref[0, 0]
    near_at = pl.ds(pl.multiple_of(even * (RIM + ROWS), RIM), RIM)
    far_at = pl.ds(pl.multiple_of((1 - even) * (RIM + ROWS), RIM), RIM)
    rims_in = [
        pltpu.make_async_copy(obs_hbm.at[0], obs.at[pl.ds(RIM, ROWS), :], rim_sem.at[0]),
        pltpu.make_async_copy(near_hbm.at[KERNELS], obs.at[near_at, :], rim_sem.at[1]),
        pltpu.make_async_copy(far_hbm.at[KERNELS], obs.at[far_at, :], rim_sem.at[2]),
        pltpu.make_async_copy(near_hbm.at[pl.ds(0, KERNELS)], coef.at[:, near_at, :], rim_sem.at[3]),
        pltpu.make_async_copy(far_hbm.at[pl.ds(0, KERNELS)], coef.at[:, far_at, :], rim_sem.at[4]),
    ]
    f_in = pltpu.make_async_copy(f_hbm, f_ref, band_sem.at[3])
    c_in = pltpu.make_async_copy(c_hbm, c_ref, band_sem.at[2])
    a_in = pltpu.make_async_copy(a_hbm, a_ref, band_sem.at[0])
    b_in = pltpu.make_async_copy(b_hbm, b_ref, band_sem.at[1])
    for copy in rims_in[:3]:
        copy.start()
    f_in.start()
    c_in.start()
    for copy in rims_in[3:]:
        copy.start()
    for k in range(KERNELS):
        coef_in(k).start()
    a_in.start()
    b_in.start()

    for r in (rb, rb2):
        r[:, :, 0:TOP, :] = jnp.zeros((2, BLOCKS, TOP, 128), BF16)
        r[:, :, TOP + LAT :, :] = jnp.zeros((2, BLOCKS, RBR - LAT - TOP, 128), BF16)
    for r in (w, w2):
        r[:, :, EXT:, :] = jnp.zeros((2, BLOCKS, WR - EXT, 128), BF16)
    acc[...] = jnp.zeros_like(acc)
    low = lax.broadcasted_iota(jnp.int32, (LAT, 128), 1) < 64
    for j in range(BLOCKS):
        sky[j] = strip_ref[128 * j : 128 * j + 128, :].astype(F32).T[:LAT]
    zero = jnp.zeros((LAT, 128), F32)
    for j in range(BLOCKS):
        after = sky[j + 1] if j + 1 < BLOCKS else zero
        before = sky[j - 1] if j > 0 else zero
        windows[j, :, 0:128] = sky[j].astype(BF16)
        windows[j, :, 128:256] = jnp.where(low, after, before).astype(BF16)
    for copy in rims_in[:3]:
        copy.wait()
    pred[...] = -obs[...].astype(F32)
    for copy in rims_in[3:]:
        copy.wait()
    f_in.wait()
    c_in.wait()

    def blur(i, rb):
        f = f_ref[i]
        for j in range(BLOCKS):
            both = dot(windows[j], f)
            rb[0, j, TOP : TOP + LAT, :] = both[:, :128].astype(BF16)
            rb[1, j, TOP : TOP + LAT, :] = both[:, 128:].astype(BF16)

    def predict(i, rb):
        for q in range(2):
            k = 2 * i + q
            c = c_ref[k]
            for h in range(2):
                out = slice(HOUT * h, HOUT * h + HOUT)
                for x in range(0, BLOCKS, 2):
                    at = slice(HOUT * h, HOUT * h + 256)
                    v = dot(c, jnp.concatenate([rb[q, x, at, :], rb[q, x + 1, at, :]], axis=1))
                    cols = slice(128 * x, 128 * x + 256)
                    pred[out, cols] += coef[k, out, cols].astype(F32) * v

    def forward(n, carry):
        for m in range(4):
            coef_in(4 * n + m).wait()
        blur(2 * n, rb)
        blur(2 * n + 1, rb2)
        predict(2 * n, rb)
        predict(2 * n + 1, rb2)
        return carry

    lax.fori_loop(0, PAIRS // 2, forward, 0)

    mask = column_of(valid_ref[...].astype(F32))
    for j in range(BLOCKS):
        pred[RIM : RIM + ROWS, 128 * j : 128 * j + 128] *= mask
    res_out = pltpu.make_async_copy(pred.at[pl.ds(RIM, ROWS), :], res_hbm.at[0], rim_sem.at[0])
    res_out.start()

    low_y = lax.broadcasted_iota(jnp.int32, (ROWS, 128), 1) < 64
    none = jnp.zeros((ROWS, 128), BF16)

    def weigh(i, w):
        for q in range(2):
            for x in range(BLOCKS):
                cols = slice(128 * x, 128 * x + 128)
                w[q, x, 0:EXT, :] = (coef[2 * i + q, :, cols].astype(F32) * pred[:, cols]).astype(BF16)

    def back(i, w, cb):
        for q in range(2):
            a = a_ref[2 * i + q]
            for h in range(2):
                for x in range(0, BLOCKS, 2):
                    at = slice(128 * h, 128 * h + 256)
                    both = dot(a, jnp.concatenate([w[q, x, at, :], w[q, x + 1, at, :]], axis=1))
                    cb[q, x, 128 * h : 128 * h + 128, :] = both[:, :128].astype(BF16)
                    cb[q, x + 1, 128 * h : 128 * h + 128, :] = both[:, 128:].astype(BF16)
        b = b_ref[i]
        for x in range(0, BLOCKS, 2):
            parts = [cb[0, x], cb[0, x + 1], cb[1, x], cb[1, x + 1]]
            for q in range(2):
                after = cb[q, x + 2] if x + 2 < BLOCKS else none
                before = cb[q, x - 1] if x > 0 else none
                parts.append(jnp.where(low_y, after, before))
            acc[x // 2] += dot(jnp.concatenate(parts, axis=1), b)

    weigh(0, w)
    a_in.wait()
    b_in.wait()

    def adjoint(n, carry):
        weigh(2 * n + 1, w2)
        back(2 * n, w, cb)
        weigh(jnp.minimum(2 * n + 2, PAIRS - 1), w)
        back(2 * n + 1, w2, cb2)
        return carry

    lax.fori_loop(0, PAIRS // 2, adjoint, 0)
    for x in range(BLOCKS // 2):
        send_ref[256 * x : 256 * x + 256, :] = acc[x].T.astype(BF16)
    res_out.wait()


def main(even, strip, valid, bands, coefficients, observed, near, far):
    return pl.pallas_call(
        main_kernel,
        out_shape=(
            jax.ShapeDtypeStruct((1, ROWS, COLS), F32),
            jax.ShapeDtypeStruct((COLS, ROWS), BF16),
        ),
        in_specs=[SMEM] + [VMEM] * 2 + [HBM] * 6 + [VMEM] * 2,
        out_specs=(ANY, VMEM),
        scratch_shapes=[
            pltpu.VMEM((PAIRS, 256, 256), BF16),
            pltpu.VMEM((KERNELS, HOUT, 256), BF16),
            pltpu.VMEM((KERNELS, 128, 256), BF16),
            pltpu.VMEM((PAIRS, 768, 256), BF16),
            pltpu.VMEM((BLOCKS, LAT, 128), F32),
            pltpu.VMEM((BLOCKS, LAT, 256), BF16),
            pltpu.VMEM((KERNELS, EXT, COLS), BF16),
            pltpu.VMEM((EXT, COLS), BF16),
            pltpu.VMEM((2, BLOCKS, RBR, 128), BF16),
            pltpu.VMEM((2, BLOCKS, RBR, 128), BF16),
            pltpu.VMEM((EXT, COLS), F32),
            pltpu.VMEM((2, BLOCKS, WR, 128), BF16),
            pltpu.VMEM((2, BLOCKS, WR, 128), BF16),
            pltpu.VMEM((2, BLOCKS, ROWS, 128), BF16),
            pltpu.VMEM((2, BLOCKS, ROWS, 128), BF16),
            pltpu.VMEM((BLOCKS // 2, ROWS, 256), F32),
            pltpu.SemaphoreType.DMA((KERNELS,)),
            pltpu.SemaphoreType.DMA((5,)),
            pltpu.SemaphoreType.DMA((4,)),
        ],
        compiler_params=pltpu.CompilerParams(vmem_limit_bytes=56 << 20),
        name="main",
    )(even, strip, valid, *bands, coefficients, observed, near, far)


def gather_kernel(cell_ref, terms_ref, out_ref):
    out_ref[...] = jnp.zeros_like(out_ref)
    for e in range(EXPOSURES):
        out_ref[cell_ref[0, e]] += terms_ref[e].astype(F32)


def gather(cell_of, terms):
    return pl.pallas_call(
        gather_kernel,
        out_shape=jax.ShapeDtypeStruct((CELLS, OWN, ROWS), F32),
        in_specs=[SMEM, VMEM],
        out_specs=VMEM,
        name="gather",
    )(cell_of, terms)


def keep(*arrays):
    return [pltpu.with_memory_space_constraint(a, pltpu.VMEM) for a in arrays]


def body(latent, row_taps, column_taps, coefficients, observed, cell_of, valid_rows):
    count = lax.axis_size("row")
    even = 1 - lax.rem(lax.axis_index("row"), 2)
    chip = [(i, i ^ 1) for i in range(count)]
    across = [(i, i + 1) for i in range(1, count - 1, 2)] + [(i + 1, i) for i in range(1, count - 1, 2)]
    cell_of = cell_of.reshape(1, EXPOSURES)
    latent = jnp.swapaxes(latent, 1, 2)

    def rim(start):
        coef = lax.dynamic_slice_in_dim(coefficients[0], start, RIM, 1)
        seen = lax.dynamic_slice_in_dim(observed, start, RIM, 1)
        usable = lax.dynamic_slice_in_dim(valid_rows[0], start, RIM, 0).astype(BF16)
        return jnp.concatenate([coef, seen], axis=0) * usable[None, :, None]

    far_sky = lax.ppermute(latent, "row", across)
    near_sky = lax.ppermute(latent, "row", chip)
    far_rim = rim((1 - even) * (ROWS - RIM))
    near_rim = rim(even * (ROWS - RIM))
    far_rim = lax.ppermute(far_rim, "row", across)
    near_rim = lax.ppermute(near_rim, "row", chip)
    even = even.reshape(1, 1)
    packed = pack(even, cell_of, latent, *keep(near_sky, far_sky))
    strip = lax.all_to_all(packed, "exp", 0, 0, tiled=True)
    f, c, a, b = make_bands(row_taps, column_taps)
    strip = strip.reshape(COLS, LATP)
    residual, send = main(
        even, *keep(strip), valid_rows, (f, c, a, b), coefficients, observed, *keep(near_rim, far_rim)
    )
    terms = lax.all_to_all(send.reshape(EXPOSURES, OWN, ROWS), "exp", 0, 0, tiled=True)
    return jnp.swapaxes(gather(cell_of, *keep(terms)), 1, 2), residual


def solution(mesh):
    placed = (
        P(None, "row", "exp"),
        P(),
        P(),
        P("exp", None, "row", None),
        P("exp", "row", None),
        P(),
        P("exp", "row"),
    )
    return jax.shard_map(
        body,
        mesh=mesh,
        in_specs=placed,
        out_specs=(P(None, "row", "exp"), P("exp", "row", None)),
        check_vma=False,
    )
```

```python
import jax
import jax.numpy as jnp
from jax import lax
from jax.experimental import pallas as pl
from jax.experimental.pallas import tpu as pltpu
from jax.sharding import PartitionSpec as P


F32 = jnp.float32
BF16 = jnp.bfloat16
KERNELS = 16
PAIRS = KERNELS // 2
TAPS = 21
HALF = TAPS // 2
CELLS = 4
EXPOSURES = 32
ROWS = 256
COLS = 1024
BLOCKS = COLS // 128
OWN = COLS // EXPOSURES
SKY = 24
RIM = 16
LAT = ROWS + 2 * SKY
EXT = ROWS + 2 * RIM
HOUT = EXT // 2
RBR = ROWS // 2 + 256
LEAD = 32
WR = HOUT + 256
EDGE = 8

VMEM = pl.BlockSpec(memory_space=pltpu.VMEM)
SMEM = pl.BlockSpec(memory_space=pltpu.SMEM)
ANY = pl.BlockSpec(memory_space=pl.ANY)
HBM = pl.BlockSpec(memory_space=pltpu.HBM)


def dot(a, b):
    return lax.dot_general(a, b, (((1,), (0,)), ((), ())), preferred_element_type=F32)


def column_of(valid):
    return jnp.broadcast_to(valid, (128, valid.shape[1])).T


def pack_kernel(even_ref, cell_ref, lat_ref, near_ref, far_ref, out_ref, turned):
    even = even_ref[0, 0] > 0
    fill = jnp.zeros((OWN, 64 - 2 * SKY), F32)
    for c in range(CELLS):
        near, far = near_ref[c].astype(F32), far_ref[c].astype(F32)
        above = jnp.where(even, far[:, ROWS - SKY :], near[:, ROWS - SKY :])
        below = jnp.where(even, near[:, :SKY], far[:, :SKY])
        edges = jnp.concatenate([above, below, fill], axis=1)
        turned[c, 0:OWN, :] = lat_ref[c]
        turned[c, OWN:, :] = jnp.concatenate(
            [edges[EDGE * g : EDGE * g + EDGE] for g in range(OWN // EDGE)], axis=1
        ).astype(BF16)
    for e in range(EXPOSURES):
        out_ref[e] = turned[cell_ref[0, e]]


def pack(even, cell_of, latent, near, far):
    return pl.pallas_call(
        pack_kernel,
        out_shape=jax.ShapeDtypeStruct((EXPOSURES, OWN + EDGE, ROWS), BF16),
        in_specs=[SMEM, SMEM, VMEM, VMEM, VMEM],
        out_specs=VMEM,
        scratch_shapes=[pltpu.VMEM((CELLS, OWN + EDGE, ROWS), BF16)],
        name="pack",
    )(even, cell_of, latent, near, far)


def base_rows(taps, place):
    lane = lax.broadcasted_iota(jnp.int32, (KERNELS, 256), 1)
    out = jnp.zeros((KERNELS, 256), F32)
    for t in range(TAPS):
        out = jnp.where(lane == place(t) % 256, taps[:, t : t + 1], out)
    return out


def skewed(row, count):
    return pltpu.roll(jnp.broadcast_to(row, (count, 256)), 0, 1, stride=1, stride_axis=0)


def bands_kernel(row_ref, col_ref, f_ref, c_hbm, a_hbm, b_hbm, c_ref, a_ref, b_ref, sem):
    c_out = pltpu.make_async_copy(c_ref, c_hbm, sem.at[PAIRS + 1])
    a_out = pltpu.make_async_copy(a_ref, a_hbm, sem.at[PAIRS])
    b_out = [pltpu.make_async_copy(b_ref.at[i], b_hbm.at[i], sem.at[i]) for i in range(PAIRS)]
    rows = row_ref[...].astype(F32)
    cols = col_ref[...].astype(F32)
    f_base = base_rows(rows, lambda t: HALF - t)
    b_base = base_rows(rows, lambda t: t - HALF)
    c_base = base_rows(cols, lambda t: t + SKY - HALF)
    a_base = base_rows(cols, lambda t: LEAD - RIM + HALF - t)
    at = lax.broadcasted_iota(jnp.int32, (256, 256), 0)
    out = lax.broadcasted_iota(jnp.int32, (256, 256), 1)
    near = jnp.abs(at - out) < 128
    for k in range(KERNELS):
        i, q = k // 2, k % 2
        f_ref[i, :, 128 * q : 128 * q + 128] = skewed(f_base[k : k + 1], 256)[:, :128].astype(BF16)
        b = skewed(b_base[k : k + 1], 256)
        b_ref[i, 256 * q : 256 * q + 256, :] = jnp.where(near, b, 0.0).astype(BF16)
        far = jnp.where(near, 0.0, b).astype(BF16)
        b_ref[i, 512 + 128 * q : 576 + 128 * q, :] = far[:64]
        b_ref[i, 576 + 128 * q : 640 + 128 * q, :] = far[192:]
        c_ref[k] = skewed(c_base[k : k + 1], 128).astype(BF16)
        a_ref[k] = skewed(a_base[k : k + 1], HOUT).astype(BF16)
        if q == 1:
            b_out[i].start()
    c_out.start()
    a_out.start()
    for copy in (*b_out, c_out, a_out):
        copy.wait()


def make_bands(row_taps, column_taps):
    return pl.pallas_call(
        bands_kernel,
        out_shape=(
            jax.ShapeDtypeStruct((PAIRS, 256, 256), BF16),
            jax.ShapeDtypeStruct((KERNELS, 128, 256), BF16),
            jax.ShapeDtypeStruct((KERNELS, HOUT, 256), BF16),
            jax.ShapeDtypeStruct((PAIRS, 768, 256), BF16),
        ),
        in_specs=[VMEM, VMEM],
        out_specs=(VMEM, HBM, HBM, HBM),
        scratch_shapes=[
            pltpu.VMEM((KERNELS, 128, 256), BF16),
            pltpu.VMEM((KERNELS, HOUT, 256), BF16),
            pltpu.VMEM((PAIRS, 768, 256), BF16),
            pltpu.SemaphoreType.DMA((PAIRS + 2,)),
        ],
        compiler_params=pltpu.CompilerParams(vmem_limit_bytes=56 << 20),
        name="bands",
    )(row_taps, column_taps)


def main_kernel(
    even_ref, strip_ref, valid_ref, f_hbm, c_hbm, a_hbm, b_hbm, coef_hbm, obs_hbm,
    res_hbm, term_ref, near_ref, far_ref,
    f_ref, c_ref, a_ref, b_ref, sky, windows, coef, obs, rb, rb2, pred, w, w2, cb, cb2, acc, sem, band_sem,
):
    def coef_in(k):
        return pltpu.make_async_copy(coef_hbm.at[0, k], coef.at[k], sem.at[k])

    pairs = ((f_hbm, f_ref), (c_hbm, c_ref), (obs_hbm.at[0], obs), (a_hbm, a_ref), (b_hbm, b_ref))
    first = [pltpu.make_async_copy(s, d, band_sem.at[n]) for n, (s, d) in enumerate(pairs)]
    for copy in first[:3]:
        copy.start()
    for k in range(KERNELS):
        coef_in(k).start()
    for copy in first[3:]:
        copy.start()

    for r in (rb, rb2):
        r[:, :, LAT:, :] = jnp.zeros((2, BLOCKS, RBR - LAT, 128), BF16)
    for r in (w, w2):
        r[:, :, 0:LEAD, :] = jnp.zeros((2, BLOCKS, LEAD, 128), BF16)
        r[:, :, LEAD + ROWS :, :] = jnp.zeros((2, BLOCKS, WR - LEAD - ROWS, 128), BF16)
    acc[...] = jnp.zeros_like(acc)
    low = lax.broadcasted_iota(jnp.int32, (LAT, 128), 1) < 64
    for j in range(BLOCKS):
        own, edges = [], []
        for e in range(4 * j, 4 * j + 4):
            own.append(strip_ref[e, 0:OWN, :].astype(F32))
            edge = strip_ref[e, OWN:, :].astype(F32)
            edges += [edge[:, 64 * g : 64 * g + 64] for g in range(OWN // EDGE)]
        edges = jnp.concatenate(edges, axis=0).T
        sky[j, 0:SKY, :] = edges[0:SKY]
        sky[j, SKY : SKY + ROWS, :] = jnp.concatenate(own, axis=0).T
        sky[j, SKY + ROWS :, :] = edges[SKY : 2 * SKY]
    zero = jnp.zeros((LAT, 128), F32)
    for j in range(BLOCKS):
        after = sky[j + 1] if j + 1 < BLOCKS else zero
        before = sky[j - 1] if j > 0 else zero
        windows[j, :, 0:128] = sky[j].astype(BF16)
        windows[j, :, 128:256] = jnp.where(low, after, before).astype(BF16)
    for copy in first[:3]:
        copy.wait()
    pred[...] = -obs[...].astype(F32)

    def blur(i, rb):
        f = f_ref[i]
        for j in range(BLOCKS):
            both = dot(windows[j], f)
            rb[0, j, 0:LAT, :] = both[:, :128].astype(BF16)
            rb[1, j, 0:LAT, :] = both[:, 128:].astype(BF16)

    def predict(i, rb):
        for q in range(2):
            k = 2 * i + q
            c = c_ref[k]
            for h in range(2):
                out = slice(128 * h, 128 * h + 128)
                for x in range(0, BLOCKS, 2):
                    at = slice(128 * h, 128 * h + 256)
                    v = dot(c, jnp.concatenate([rb[q, x, at, :], rb[q, x + 1, at, :]], axis=1))
                    cols = slice(128 * x, 128 * x + 256)
                    pred[out, cols] += coef[k, out, cols].astype(F32) * v

    def forward(n, carry):
        for m in range(4):
            coef_in(4 * n + m).wait()
        blur(2 * n, rb)
        blur(2 * n + 1, rb2)
        predict(2 * n, rb)
        predict(2 * n + 1, rb2)
        return carry

    lax.fori_loop(0, PAIRS // 2, forward, 0)

    mask = column_of(valid_ref[...].astype(F32))
    for j in range(BLOCKS):
        pred[:, 128 * j : 128 * j + 128] *= mask
    res_out = pltpu.make_async_copy(pred, res_hbm.at[0], band_sem.at[0])
    res_out.start()

    low_y = lax.broadcasted_iota(jnp.int32, (EXT, 128), 1) < 64
    none = jnp.zeros((EXT, 128), BF16)

    def weigh(i, w):
        for q in range(2):
            for x in range(BLOCKS):
                cols = slice(128 * x, 128 * x + 128)
                w[q, x, LEAD : LEAD + ROWS, :] = (coef[2 * i + q, :, cols].astype(F32) * pred[:, cols]).astype(BF16)

    def back(i, w, cb):
        for q in range(2):
            a = a_ref[2 * i + q]
            for h in range(2):
                out = slice(HOUT * h, HOUT * h + HOUT)
                at = slice(HOUT * h, HOUT * h + 256)
                for x in range(0, BLOCKS, 2):
                    both = dot(a, jnp.concatenate([w[q, x, at, :], w[q, x + 1, at, :]], axis=1))
                    cb[q, x, out, :] = both[:, :128].astype(BF16)
                    cb[q, x + 1, out, :] = both[:, 128:].astype(BF16)
        b = b_ref[i]
        for x in range(0, BLOCKS, 2):
            parts = [cb[0, x], cb[0, x + 1], cb[1, x], cb[1, x + 1]]
            for q in range(2):
                after = cb[q, x + 2] if x + 2 < BLOCKS else none
                before = cb[q, x - 1] if x > 0 else none
                parts.append(jnp.where(low_y, after, before))
            acc[x // 2] += dot(jnp.concatenate(parts, axis=1), b)

    weigh(0, w)
    for copy in first[3:]:
        copy.wait()

    def adjoint(n, carry):
        weigh(2 * n + 1, w2)
        back(2 * n, w, cb)
        weigh(jnp.minimum(2 * n + 2, PAIRS - 1), w)
        back(2 * n + 1, w2, cb2)
        return carry

    lax.fori_loop(0, PAIRS // 2, adjoint, 0)
    even = even_ref[0, 0] > 0
    for x in range(BLOCKS // 2):
        head, tail = acc[x, 0:RIM, :], acc[x, RIM + ROWS :, :]
        near_ref[x] = jnp.where(even, tail, head)
        far_ref[x] = jnp.where(even, head, tail)
        term_ref[x] = acc[x, RIM : RIM + ROWS, :]
    res_out.wait()


def main(even, strip, valid, bands, coefficients, observed):
    rim = jax.ShapeDtypeStruct((BLOCKS // 2, RIM, 256), F32)
    return pl.pallas_call(
        main_kernel,
        out_shape=(
            jax.ShapeDtypeStruct((1, ROWS, COLS), F32),
            jax.ShapeDtypeStruct((BLOCKS // 2, ROWS, 256), F32),
            rim,
            rim,
        ),
        in_specs=[SMEM] + [VMEM] * 2 + [HBM] * 6,
        out_specs=(HBM, VMEM, VMEM, VMEM),
        scratch_shapes=[
            pltpu.VMEM((PAIRS, 256, 256), BF16),
            pltpu.VMEM((KERNELS, 128, 256), BF16),
            pltpu.VMEM((KERNELS, HOUT, 256), BF16),
            pltpu.VMEM((PAIRS, 768, 256), BF16),
            pltpu.VMEM((BLOCKS, LAT, 128), F32),
            pltpu.VMEM((BLOCKS, LAT, 256), BF16),
            pltpu.VMEM((KERNELS, ROWS, COLS), BF16),
            pltpu.VMEM((ROWS, COLS), BF16),
            pltpu.VMEM((2, BLOCKS, RBR, 128), BF16),
            pltpu.VMEM((2, BLOCKS, RBR, 128), BF16),
            pltpu.VMEM((ROWS, COLS), F32),
            pltpu.VMEM((2, BLOCKS, WR, 128), BF16),
            pltpu.VMEM((2, BLOCKS, WR, 128), BF16),
            pltpu.VMEM((2, BLOCKS, EXT, 128), BF16),
            pltpu.VMEM((2, BLOCKS, EXT, 128), BF16),
            pltpu.VMEM((BLOCKS // 2, EXT, 256), F32),
            pltpu.SemaphoreType.DMA((KERNELS,)),
            pltpu.SemaphoreType.DMA((5,)),
        ],
        compiler_params=pltpu.CompilerParams(vmem_limit_bytes=56 << 20),
        name="main",
    )(even, strip, valid, *bands, coefficients, observed)


def finish_kernel(even_ref, term_ref, near_ref, far_ref, send_ref):
    even = even_ref[0, 0] > 0
    for x in range(BLOCKS // 2):
        near, far = near_ref[x], far_ref[x]
        top = term_ref[x, 0:RIM, :] + jnp.where(even, far, near)
        bottom = term_ref[x, ROWS - RIM :, :] + jnp.where(even, near, far)
        whole = jnp.concatenate([top, term_ref[x, RIM : ROWS - RIM, :], bottom], axis=0)
        send_ref[256 * x : 256 * x + 256, :] = whole.T.astype(BF16)


def finish(even, term, near, far):
    return pl.pallas_call(
        finish_kernel,
        out_shape=jax.ShapeDtypeStruct((COLS, ROWS), BF16),
        in_specs=[SMEM, VMEM, VMEM, VMEM],
        out_specs=VMEM,
        name="finish",
    )(even, term, near, far)


def gather_kernel(cell_ref, terms_ref, out_ref):
    out_ref[...] = jnp.zeros_like(out_ref)
    for e in range(EXPOSURES):
        out_ref[cell_ref[0, e]] += terms_ref[e].astype(F32)


def gather(cell_of, terms):
    return pl.pallas_call(
        gather_kernel,
        out_shape=jax.ShapeDtypeStruct((CELLS, OWN, ROWS), F32),
        in_specs=[SMEM, VMEM],
        out_specs=VMEM,
        name="gather",
    )(cell_of, terms)


def keep(*arrays):
    return [pltpu.with_memory_space_constraint(a, pltpu.VMEM) for a in arrays]


def body(latent, row_taps, column_taps, coefficients, observed, cell_of, valid_rows):
    count = lax.axis_size("row")
    even = 1 - lax.rem(lax.axis_index("row"), 2)
    chip = [(i, i ^ 1) for i in range(count)]
    across = [(i, i + 1) for i in range(1, count - 1, 2)] + [(i + 1, i) for i in range(1, count - 1, 2)]
    cell_of = cell_of.reshape(1, EXPOSURES)
    latent = jnp.swapaxes(latent, 1, 2)

    far_sky = lax.ppermute(latent, "row", across)
    near_sky = lax.ppermute(latent, "row", chip)
    even = even.reshape(1, 1)
    packed = pack(even, cell_of, latent, *keep(near_sky, far_sky))
    strip = lax.all_to_all(packed, "exp", 0, 0, tiled=True)
    bands = make_bands(row_taps, column_taps)
    residual, *terms = main(even, *keep(strip), valid_rows, bands, coefficients, observed)
    term, near, far = keep(*terms)
    far = lax.ppermute(far, "row", across)
    near = lax.ppermute(near, "row", chip)
    send = finish(even, *keep(term, near, far)).reshape(EXPOSURES, OWN, ROWS)
    terms = lax.all_to_all(send, "exp", 0, 0, tiled=True)
    return jnp.swapaxes(gather(cell_of, *keep(terms)), 1, 2), residual


def solution(mesh):
    placed = (
        P(None, "row", "exp"),
        P(),
        P(),
        P("exp", None, "row", None),
        P("exp", "row", None),
        P(),
        P("exp", "row"),
    )
    return jax.shard_map(
        body,
        mesh=mesh,
        in_specs=placed,
        out_specs=(P(None, "row", "exp"), P("exp", "row", None)),
        check_vma=False,
    )
```

```python
import jax
import jax.numpy as jnp
from jax import lax
from jax.experimental import pallas as pl
from jax.experimental.pallas import tpu as pltpu
from jax.sharding import PartitionSpec as P


F32 = jnp.float32
BF16 = jnp.bfloat16
KERNELS = 16
PAIRS = KERNELS // 2
TAPS = 21
HALF = TAPS // 2
CELLS = 4
EXPOSURES = 32
ROWS = 256
COLS = 1024
BLOCKS = COLS // 128
OWN = COLS // EXPOSURES
SKY = 24
RIM = 16
LAT = ROWS + 2 * SKY
EDGE = 8
EXT = ROWS + 2 * RIM
HOUT = EXT // 2
TOP = 8
RBR = HOUT + 256
WR = 384

VMEM = pl.BlockSpec(memory_space=pltpu.VMEM)
SMEM = pl.BlockSpec(memory_space=pltpu.SMEM)
ANY = pl.BlockSpec(memory_space=pl.ANY)
HBM = pl.BlockSpec(memory_space=pltpu.HBM)


def dot(a, b):
    return lax.dot_general(a, b, (((1,), (0,)), ((), ())), preferred_element_type=F32)


def column_of(valid):
    return jnp.broadcast_to(valid, (128, valid.shape[1])).T


def pack_kernel(even_ref, cell_ref, lat_ref, near_ref, far_ref, out_ref, turned):
    even = even_ref[0, 0] > 0
    fill = jnp.zeros((OWN, 64 - 2 * SKY), F32)
    for c in range(CELLS):
        near, far = near_ref[c].astype(F32), far_ref[c].astype(F32)
        above = jnp.where(even, far[:, ROWS - SKY :], near[:, ROWS - SKY :])
        below = jnp.where(even, near[:, :SKY], far[:, :SKY])
        edges = jnp.concatenate([above, below, fill], axis=1)
        turned[c, 0:OWN, :] = lat_ref[c]
        turned[c, OWN:, :] = jnp.concatenate(
            [edges[EDGE * g : EDGE * g + EDGE] for g in range(OWN // EDGE)], axis=1
        ).astype(BF16)
    for e in range(EXPOSURES):
        out_ref[e] = turned[cell_ref[0, e]]


def pack(even, cell_of, latent, near, far):
    return pl.pallas_call(
        pack_kernel,
        out_shape=jax.ShapeDtypeStruct((EXPOSURES, OWN + EDGE, ROWS), BF16),
        in_specs=[SMEM, SMEM, VMEM, VMEM, VMEM],
        out_specs=VMEM,
        scratch_shapes=[pltpu.VMEM((CELLS, OWN + EDGE, ROWS), BF16)],
        name="pack",
    )(even, cell_of, latent, near, far)


def base_rows(taps, place):
    lane = lax.broadcasted_iota(jnp.int32, (KERNELS, 256), 1)
    out = jnp.zeros((KERNELS, 256), F32)
    for t in range(TAPS):
        out = jnp.where(lane == place(t) % 256, taps[:, t : t + 1], out)
    return out


def skewed(row, count):
    return pltpu.roll(jnp.broadcast_to(row, (count, 256)), 0, 1, stride=1, stride_axis=0)


def bands_kernel(row_ref, col_ref, f_ref, c_hbm, a_hbm, b_hbm, c_ref, a_ref, b_ref, sem):
    c_out = pltpu.make_async_copy(c_ref, c_hbm, sem.at[PAIRS + 1])
    a_out = pltpu.make_async_copy(a_ref, a_hbm, sem.at[PAIRS])
    b_out = [pltpu.make_async_copy(b_ref.at[i], b_hbm.at[i], sem.at[i]) for i in range(PAIRS)]
    rows = row_ref[...].astype(F32)
    cols = col_ref[...].astype(F32)
    f_base = base_rows(rows, lambda t: HALF - t)
    b_base = base_rows(rows, lambda t: t - HALF)
    c_base = base_rows(cols, lambda t: t + 2 * RIM - RIM - HALF)
    a_base = base_rows(cols, lambda t: RIM + HALF - t)
    at = lax.broadcasted_iota(jnp.int32, (256, 256), 0)
    out = lax.broadcasted_iota(jnp.int32, (256, 256), 1)
    near = jnp.abs(at - out) < 128
    for k in range(KERNELS):
        i, q = k // 2, k % 2
        f_ref[i, :, 128 * q : 128 * q + 128] = skewed(f_base[k : k + 1], 256)[:, :128].astype(BF16)
        b = skewed(b_base[k : k + 1], 256)
        b_ref[i, 256 * q : 256 * q + 256, :] = jnp.where(near, b, 0.0).astype(BF16)
        far = jnp.where(near, 0.0, b).astype(BF16)
        b_ref[i, 512 + 128 * q : 576 + 128 * q, :] = far[:64]
        b_ref[i, 576 + 128 * q : 640 + 128 * q, :] = far[192:]
        c_ref[k] = skewed(c_base[k : k + 1], HOUT).astype(BF16)
        a_ref[k] = skewed(a_base[k : k + 1], 128).astype(BF16)
        if q == 1:
            b_out[i].start()
    c_out.start()
    a_out.start()
    for copy in (*b_out, c_out, a_out):
        copy.wait()


def make_bands(row_taps, column_taps):
    return pl.pallas_call(
        bands_kernel,
        out_shape=(
            jax.ShapeDtypeStruct((PAIRS, 256, 256), BF16),
            jax.ShapeDtypeStruct((KERNELS, HOUT, 256), BF16),
            jax.ShapeDtypeStruct((KERNELS, 128, 256), BF16),
            jax.ShapeDtypeStruct((PAIRS, 768, 256), BF16),
        ),
        in_specs=[VMEM, VMEM],
        out_specs=(VMEM, HBM, HBM, HBM),
        scratch_shapes=[
            pltpu.VMEM((KERNELS, HOUT, 256), BF16),
            pltpu.VMEM((KERNELS, 128, 256), BF16),
            pltpu.VMEM((PAIRS, 768, 256), BF16),
            pltpu.SemaphoreType.DMA((PAIRS + 2,)),
        ],
        compiler_params=pltpu.CompilerParams(vmem_limit_bytes=56 << 20),
        name="bands",
    )(row_taps, column_taps)


def main_kernel(
    even_ref, strip_ref, valid_ref, f_hbm, c_hbm, a_hbm, b_hbm, coef_hbm, obs_hbm, near_hbm, far_hbm,
    res_hbm, send_ref,
    f_ref, c_ref, a_ref, b_ref, sky, windows, coef, obs, rb, rb2, pred, w, w2, cb, cb2, acc, sem, rim_sem, band_sem,
):
    def coef_in(k):
        return pltpu.make_async_copy(coef_hbm.at[0, k], coef.at[k, pl.ds(RIM, ROWS), :], sem.at[k])

    even = even_ref[0, 0]
    near_at = pl.ds(pl.multiple_of(even * (RIM + ROWS), RIM), RIM)
    far_at = pl.ds(pl.multiple_of((1 - even) * (RIM + ROWS), RIM), RIM)
    rims_in = [
        pltpu.make_async_copy(obs_hbm.at[0], obs.at[pl.ds(RIM, ROWS), :], rim_sem.at[0]),
        pltpu.make_async_copy(near_hbm.at[KERNELS], obs.at[near_at, :], rim_sem.at[1]),
        pltpu.make_async_copy(far_hbm.at[KERNELS], obs.at[far_at, :], rim_sem.at[2]),
        pltpu.make_async_copy(near_hbm.at[pl.ds(0, KERNELS)], coef.at[:, near_at, :], rim_sem.at[3]),
        pltpu.make_async_copy(far_hbm.at[pl.ds(0, KERNELS)], coef.at[:, far_at, :], rim_sem.at[4]),
    ]
    f_in = pltpu.make_async_copy(f_hbm, f_ref, band_sem.at[3])
    c_in = pltpu.make_async_copy(c_hbm, c_ref, band_sem.at[2])
    a_in = pltpu.make_async_copy(a_hbm, a_ref, band_sem.at[0])
    b_in = pltpu.make_async_copy(b_hbm, b_ref, band_sem.at[1])
    for copy in rims_in[:3]:
        copy.start()
    f_in.start()
    c_in.start()
    for copy in rims_in[3:]:
        copy.start()
    for k in range(KERNELS):
        coef_in(k).start()
    a_in.start()
    b_in.start()

    for r in (rb, rb2):
        r[:, :, 0:TOP, :] = jnp.zeros((2, BLOCKS, TOP, 128), BF16)
        r[:, :, TOP + LAT :, :] = jnp.zeros((2, BLOCKS, RBR - LAT - TOP, 128), BF16)
    for r in (w, w2):
        r[:, :, EXT:, :] = jnp.zeros((2, BLOCKS, WR - EXT, 128), BF16)
    acc[...] = jnp.zeros_like(acc)
    low = lax.broadcasted_iota(jnp.int32, (LAT, 128), 1) < 64
    for j in range(BLOCKS):
        own, edges = [], []
        for e in range(4 * j, 4 * j + 4):
            own.append(strip_ref[e, 0:OWN, :].astype(F32))
            edge = strip_ref[e, OWN:, :].astype(F32)
            edges += [edge[:, 64 * g : 64 * g + 64] for g in range(OWN // EDGE)]
        edges = jnp.concatenate(edges, axis=0).T
        sky[j, 0:SKY, :] = edges[0:SKY]
        sky[j, SKY : SKY + ROWS, :] = jnp.concatenate(own, axis=0).T
        sky[j, SKY + ROWS :, :] = edges[SKY : 2 * SKY]
    zero = jnp.zeros((LAT, 128), F32)
    for j in range(BLOCKS):
        after = sky[j + 1] if j + 1 < BLOCKS else zero
        before = sky[j - 1] if j > 0 else zero
        windows[j, :, 0:128] = sky[j].astype(BF16)
        windows[j, :, 128:256] = jnp.where(low, after, before).astype(BF16)
    for copy in rims_in[:3]:
        copy.wait()
    pred[...] = -obs[...].astype(F32)
    for copy in rims_in[3:]:
        copy.wait()
    f_in.wait()
    c_in.wait()

    def blur(i, rb):
        f = f_ref[i]
        for j in range(BLOCKS):
            both = dot(windows[j], f)
            rb[0, j, TOP : TOP + LAT, :] = both[:, :128].astype(BF16)
            rb[1, j, TOP : TOP + LAT, :] = both[:, 128:].astype(BF16)

    def predict(i, rb):
        for q in range(2):
            k = 2 * i + q
            c = c_ref[k]
            for h in range(2):
                out = slice(HOUT * h, HOUT * h + HOUT)
                for x in range(0, BLOCKS, 2):
                    at = slice(HOUT * h, HOUT * h + 256)
                    v = dot(c, jnp.concatenate([rb[q, x, at, :], rb[q, x + 1, at, :]], axis=1))
                    cols = slice(128 * x, 128 * x + 256)
                    pred[out, cols] += coef[k, out, cols].astype(F32) * v

    def forward(n, carry):
        for m in range(4):
            coef_in(4 * n + m).wait()
        blur(2 * n, rb)
        blur(2 * n + 1, rb2)
        predict(2 * n, rb)
        predict(2 * n + 1, rb2)
        return carry

    lax.fori_loop(0, PAIRS // 2, forward, 0)

    mask = column_of(valid_ref[...].astype(F32))
    for j in range(BLOCKS):
        pred[RIM : RIM + ROWS, 128 * j : 128 * j + 128] *= mask
    res_out = pltpu.make_async_copy(pred.at[pl.ds(RIM, ROWS), :], res_hbm.at[0], rim_sem.at[0])
    res_out.start()

    low_y = lax.broadcasted_iota(jnp.int32, (ROWS, 128), 1) < 64
    none = jnp.zeros((ROWS, 128), BF16)

    def weigh(i, w):
        for q in range(2):
            for x in range(BLOCKS):
                cols = slice(128 * x, 128 * x + 128)
                w[q, x, 0:EXT, :] = (coef[2 * i + q, :, cols].astype(F32) * pred[:, cols]).astype(BF16)

    def back(i, w, cb):
        for q in range(2):
            a = a_ref[2 * i + q]
            for h in range(2):
                for x in range(0, BLOCKS, 2):
                    at = slice(128 * h, 128 * h + 256)
                    both = dot(a, jnp.concatenate([w[q, x, at, :], w[q, x + 1, at, :]], axis=1))
                    cb[q, x, 128 * h : 128 * h + 128, :] = both[:, :128].astype(BF16)
                    cb[q, x + 1, 128 * h : 128 * h + 128, :] = both[:, 128:].astype(BF16)
        b = b_ref[i]
        for x in range(0, BLOCKS, 2):
            parts = [cb[0, x], cb[0, x + 1], cb[1, x], cb[1, x + 1]]
            for q in range(2):
                after = cb[q, x + 2] if x + 2 < BLOCKS else none
                before = cb[q, x - 1] if x > 0 else none
                parts.append(jnp.where(low_y, after, before))
            acc[x // 2] += dot(jnp.concatenate(parts, axis=1), b)

    weigh(0, w)
    a_in.wait()
    b_in.wait()

    def adjoint(n, carry):
        weigh(2 * n + 1, w2)
        back(2 * n, w, cb)
        weigh(jnp.minimum(2 * n + 2, PAIRS - 1), w)
        back(2 * n + 1, w2, cb2)
        return carry

    lax.fori_loop(0, PAIRS // 2, adjoint, 0)
    for x in range(BLOCKS // 2):
        send_ref[256 * x : 256 * x + 256, :] = acc[x].T.astype(BF16)
    res_out.wait()


def main(even, strip, valid, bands, coefficients, observed, near, far):
    return pl.pallas_call(
        main_kernel,
        out_shape=(
            jax.ShapeDtypeStruct((1, ROWS, COLS), F32),
            jax.ShapeDtypeStruct((COLS, ROWS), BF16),
        ),
        in_specs=[SMEM] + [VMEM] * 2 + [HBM] * 6 + [VMEM] * 2,
        out_specs=(ANY, VMEM),
        scratch_shapes=[
            pltpu.VMEM((PAIRS, 256, 256), BF16),
            pltpu.VMEM((KERNELS, HOUT, 256), BF16),
            pltpu.VMEM((KERNELS, 128, 256), BF16),
            pltpu.VMEM((PAIRS, 768, 256), BF16),
            pltpu.VMEM((BLOCKS, LAT, 128), F32),
            pltpu.VMEM((BLOCKS, LAT, 256), BF16),
            pltpu.VMEM((KERNELS, EXT, COLS), BF16),
            pltpu.VMEM((EXT, COLS), BF16),
            pltpu.VMEM((2, BLOCKS, RBR, 128), BF16),
            pltpu.VMEM((2, BLOCKS, RBR, 128), BF16),
            pltpu.VMEM((EXT, COLS), F32),
            pltpu.VMEM((2, BLOCKS, WR, 128), BF16),
            pltpu.VMEM((2, BLOCKS, WR, 128), BF16),
            pltpu.VMEM((2, BLOCKS, ROWS, 128), BF16),
            pltpu.VMEM((2, BLOCKS, ROWS, 128), BF16),
            pltpu.VMEM((BLOCKS // 2, ROWS, 256), F32),
            pltpu.SemaphoreType.DMA((KERNELS,)),
            pltpu.SemaphoreType.DMA((5,)),
            pltpu.SemaphoreType.DMA((4,)),
        ],
        compiler_params=pltpu.CompilerParams(vmem_limit_bytes=56 << 20),
        name="main",
    )(even, strip, valid, *bands, coefficients, observed, near, far)


def gather_kernel(cell_ref, terms_ref, out_ref):
    out_ref[...] = jnp.zeros_like(out_ref)
    for e in range(EXPOSURES):
        out_ref[cell_ref[0, e]] += terms_ref[e].astype(F32)


def gather(cell_of, terms):
    return pl.pallas_call(
        gather_kernel,
        out_shape=jax.ShapeDtypeStruct((CELLS, OWN, ROWS), F32),
        in_specs=[SMEM, VMEM],
        out_specs=VMEM,
        name="gather",
    )(cell_of, terms)


def keep(*arrays):
    return [pltpu.with_memory_space_constraint(a, pltpu.VMEM) for a in arrays]


def body(latent, row_taps, column_taps, coefficients, observed, cell_of, valid_rows):
    count = lax.axis_size("row")
    even = 1 - lax.rem(lax.axis_index("row"), 2)
    chip = [(i, i ^ 1) for i in range(count)]
    across = [(i, i + 1) for i in range(1, count - 1, 2)] + [(i + 1, i) for i in range(1, count - 1, 2)]
    cell_of = cell_of.reshape(1, EXPOSURES)
    latent = jnp.swapaxes(latent, 1, 2)

    def rim(start):
        coef = lax.dynamic_slice_in_dim(coefficients[0], start, RIM, 1)
        seen = lax.dynamic_slice_in_dim(observed, start, RIM, 1)
        usable = lax.dynamic_slice_in_dim(valid_rows[0], start, RIM, 0).astype(BF16)
        return jnp.concatenate([coef, seen], axis=0) * usable[None, :, None]

    far_sky = lax.ppermute(latent, "row", across)
    near_sky = lax.ppermute(latent, "row", chip)
    far_rim = rim((1 - even) * (ROWS - RIM))
    near_rim = rim(even * (ROWS - RIM))
    even = even.reshape(1, 1)
    packed = pack(even, cell_of, latent, *keep(near_sky, far_sky))
    strip = lax.all_to_all(packed, "exp", 0, 0, tiled=True)
    far_rim = lax.ppermute(far_rim, "row", across)
    near_rim = lax.ppermute(near_rim, "row", chip)
    f, c, a, b = make_bands(row_taps, column_taps)
    residual, send = main(
        even, *keep(strip), valid_rows, (f, c, a, b), coefficients, observed, *keep(near_rim, far_rim)
    )
    terms = lax.all_to_all(send.reshape(EXPOSURES, OWN, ROWS), "exp", 0, 0, tiled=True)
    return jnp.swapaxes(gather(cell_of, *keep(terms)), 1, 2), residual


def solution(mesh):
    placed = (
        P(None, "row", "exp"),
        P(),
        P(),
        P("exp", None, "row", None),
        P("exp", "row", None),
        P(),
        P("exp", "row"),
    )
    return jax.shard_map(
        body,
        mesh=mesh,
        in_specs=placed,
        out_specs=(P(None, "row", "exp"), P("exp", "row", None)),
        check_vma=False,
    )
```

```python
import jax
import jax.numpy as jnp
from jax import lax
from jax.experimental import pallas as pl
from jax.experimental.pallas import tpu as pltpu
from jax.sharding import PartitionSpec as P


F32 = jnp.float32
BF16 = jnp.bfloat16
KERNELS = 16
PAIRS = KERNELS // 2
TAPS = 21
HALF = TAPS // 2
CELLS = 4
EXPOSURES = 32
ROWS = 256
COLS = 1024
BLOCKS = COLS // 128
OWN = COLS // EXPOSURES
SKY = 24
RIM = 16
FULL = 8
REST = HALF - FULL
PLANES = KERNELS + 1
LAT = ROWS + 2 * SKY
EDGE = 8
EXT = ROWS + 2 * RIM
HOUT = EXT // 2
TOP = 8
RBR = HOUT + 256
WR = 384

VMEM = pl.BlockSpec(memory_space=pltpu.VMEM)
SMEM = pl.BlockSpec(memory_space=pltpu.SMEM)
ANY = pl.BlockSpec(memory_space=pl.ANY)
HBM = pl.BlockSpec(memory_space=pltpu.HBM)


def dot(a, b):
    return lax.dot_general(a, b, (((1,), (0,)), ((), ())), preferred_element_type=F32)


def column_of(valid):
    return jnp.broadcast_to(valid, (128, valid.shape[1])).T


def cut_kernel(even_ref, valid_ref, obs_hbm, coef_hbm, near_ref, far_ref, near_in, far_in, sem):
    even = even_ref[0, 0]
    outs = ((even, near_ref, near_in), (1 - even, far_ref, far_in))
    copies = []
    for n, (last, _, block) in enumerate(outs):
        rows = pl.ds(pl.multiple_of(last * (ROWS - RIM), RIM), RIM)
        copies += [
            pltpu.make_async_copy(coef_hbm.at[0, :, rows, :], block.at[pl.ds(0, KERNELS)], sem.at[2 * n]),
            pltpu.make_async_copy(obs_hbm.at[0, rows, :], block.at[KERNELS], sem.at[2 * n + 1]),
        ]
    for copy in copies:
        copy.start()
    mask = column_of(valid_ref[...].astype(F32))
    head_mask = jnp.concatenate([mask[:RIM]] * BLOCKS, axis=1)
    tail_mask = jnp.concatenate([mask[ROWS - RIM :]] * BLOCKS, axis=1)
    for copy in copies:
        copy.wait()
    for last, out, block in outs:
        tail = last > 0
        usable = jnp.where(tail, tail_mask, head_mask)
        rest = []
        for k in range(PLANES):
            rows = block[k].astype(F32) * usable
            out[k] = jnp.where(tail, rows[RIM - FULL :], rows[:FULL]).astype(BF16)
            rest.append(jnp.where(tail, rows[RIM - HALF : RIM - FULL], rows[FULL:HALF]))
        rest += [jnp.zeros((REST, COLS), F32)] * (-PLANES * REST % FULL // REST)
        for n in range(len(rest) * REST // FULL):
            each = FULL // REST
            out[PLANES + n] = jnp.concatenate(rest[each * n : each * n + each], axis=0).astype(BF16)


def cut(even, valid, observed, coefficients):
    planes = PLANES + -(-PLANES * REST // FULL)
    block = pltpu.VMEM((PLANES, RIM, COLS), BF16)
    return pl.pallas_call(
        cut_kernel,
        out_shape=(jax.ShapeDtypeStruct((planes, FULL, COLS), BF16),) * 2,
        in_specs=[SMEM, VMEM, HBM, HBM],
        out_specs=(VMEM,) * 2,
        scratch_shapes=[block, block, pltpu.SemaphoreType.DMA((4,))],
        name="cut",
    )(even, valid, observed, coefficients)


def pack_kernel(even_ref, cell_ref, lat_ref, near_ref, far_ref, out_ref, turned):
    even = even_ref[0, 0] > 0
    fill = jnp.zeros((OWN, 64 - 2 * SKY), F32)
    for c in range(CELLS):
        near, far = near_ref[c].astype(F32), far_ref[c].astype(F32)
        above = jnp.where(even, far[:, ROWS - SKY :], near[:, ROWS - SKY :])
        below = jnp.where(even, near[:, :SKY], far[:, :SKY])
        edges = jnp.concatenate([above, below, fill], axis=1)
        turned[c, 0:OWN, :] = lat_ref[c]
        turned[c, OWN:, :] = jnp.concatenate(
            [edges[EDGE * g : EDGE * g + EDGE] for g in range(OWN // EDGE)], axis=1
        ).astype(BF16)
    for e in range(EXPOSURES):
        out_ref[e] = turned[cell_ref[0, e]]


def pack(even, cell_of, latent, near, far):
    return pl.pallas_call(
        pack_kernel,
        out_shape=jax.ShapeDtypeStruct((EXPOSURES, OWN + EDGE, ROWS), BF16),
        in_specs=[SMEM, SMEM, VMEM, VMEM, VMEM],
        out_specs=VMEM,
        scratch_shapes=[pltpu.VMEM((CELLS, OWN + EDGE, ROWS), BF16)],
        name="pack",
    )(even, cell_of, latent, near, far)


def base_rows(taps, place):
    lane = lax.broadcasted_iota(jnp.int32, (KERNELS, 256), 1)
    out = jnp.zeros((KERNELS, 256), F32)
    for t in range(TAPS):
        out = jnp.where(lane == place(t) % 256, taps[:, t : t + 1], out)
    return out


def skewed(row, count):
    return pltpu.roll(jnp.broadcast_to(row, (count, 256)), 0, 1, stride=1, stride_axis=0)


def bands_kernel(row_ref, col_ref, f_ref, c_hbm, a_hbm, b_hbm, c_ref, a_ref, b_ref, sem):
    c_out = pltpu.make_async_copy(c_ref, c_hbm, sem.at[PAIRS + 1])
    a_out = pltpu.make_async_copy(a_ref, a_hbm, sem.at[PAIRS])
    b_out = [pltpu.make_async_copy(b_ref.at[i], b_hbm.at[i], sem.at[i]) for i in range(PAIRS)]
    rows = row_ref[...].astype(F32)
    cols = col_ref[...].astype(F32)
    f_base = base_rows(rows, lambda t: HALF - t)
    b_base = base_rows(rows, lambda t: t - HALF)
    c_base = base_rows(cols, lambda t: t + 2 * RIM - RIM - HALF)
    a_base = base_rows(cols, lambda t: RIM + HALF - t)
    at = lax.broadcasted_iota(jnp.int32, (256, 256), 0)
    out = lax.broadcasted_iota(jnp.int32, (256, 256), 1)
    near = jnp.abs(at - out) < 128
    for k in range(KERNELS):
        i, q = k // 2, k % 2
        f_ref[i, :, 128 * q : 128 * q + 128] = skewed(f_base[k : k + 1], 256)[:, :128].astype(BF16)
        b = skewed(b_base[k : k + 1], 256)
        b_ref[i, 256 * q : 256 * q + 256, :] = jnp.where(near, b, 0.0).astype(BF16)
        far = jnp.where(near, 0.0, b).astype(BF16)
        b_ref[i, 512 + 128 * q : 576 + 128 * q, :] = far[:64]
        b_ref[i, 576 + 128 * q : 640 + 128 * q, :] = far[192:]
        c_ref[k] = skewed(c_base[k : k + 1], HOUT).astype(BF16)
        a_ref[k] = skewed(a_base[k : k + 1], 128).astype(BF16)
        if q == 1:
            b_out[i].start()
    c_out.start()
    a_out.start()
    for copy in (*b_out, c_out, a_out):
        copy.wait()


def make_bands(row_taps, column_taps):
    return pl.pallas_call(
        bands_kernel,
        out_shape=(
            jax.ShapeDtypeStruct((PAIRS, 256, 256), BF16),
            jax.ShapeDtypeStruct((KERNELS, HOUT, 256), BF16),
            jax.ShapeDtypeStruct((KERNELS, 128, 256), BF16),
            jax.ShapeDtypeStruct((PAIRS, 768, 256), BF16),
        ),
        in_specs=[VMEM, VMEM],
        out_specs=(VMEM, HBM, HBM, HBM),
        scratch_shapes=[
            pltpu.VMEM((KERNELS, HOUT, 256), BF16),
            pltpu.VMEM((KERNELS, 128, 256), BF16),
            pltpu.VMEM((PAIRS, 768, 256), BF16),
            pltpu.SemaphoreType.DMA((PAIRS + 2,)),
        ],
        compiler_params=pltpu.CompilerParams(vmem_limit_bytes=56 << 20),
        name="bands",
    )(row_taps, column_taps)


def main_kernel(
    even_ref, strip_ref, valid_ref, f_hbm, c_hbm, a_hbm, b_hbm, coef_hbm, obs_hbm, near_ref, far_ref,
    res_hbm, send_ref,
    f_ref, c_ref, a_ref, b_ref, sky, windows, coef, obs, rb, rb2, pred, w, w2, cb, cb2, acc, sem, rim_sem, band_sem,
):
    def coef_in(k):
        return pltpu.make_async_copy(coef_hbm.at[0, k], coef.at[k, pl.ds(RIM, ROWS), :], sem.at[k])

    even = even_ref[0, 0]
    near_at = pl.ds(pl.multiple_of(FULL + even * (FULL + ROWS), FULL), FULL)
    far_at = pl.ds(pl.multiple_of(FULL + (1 - even) * (FULL + ROWS), FULL), FULL)
    rims_in = [
        pltpu.make_async_copy(obs_hbm.at[0], obs.at[pl.ds(RIM, ROWS), :], rim_sem.at[0]),
        pltpu.make_async_copy(near_ref.at[KERNELS], obs.at[near_at, :], rim_sem.at[1]),
        pltpu.make_async_copy(far_ref.at[KERNELS], obs.at[far_at, :], rim_sem.at[2]),
        pltpu.make_async_copy(near_ref.at[pl.ds(0, KERNELS)], coef.at[:, near_at, :], rim_sem.at[3]),
        pltpu.make_async_copy(far_ref.at[pl.ds(0, KERNELS)], coef.at[:, far_at, :], rim_sem.at[4]),
    ]
    f_in = pltpu.make_async_copy(f_hbm, f_ref, band_sem.at[3])
    c_in = pltpu.make_async_copy(c_hbm, c_ref, band_sem.at[2])
    a_in = pltpu.make_async_copy(a_hbm, a_ref, band_sem.at[0])
    b_in = pltpu.make_async_copy(b_hbm, b_ref, band_sem.at[1])
    for copy in rims_in[:3]:
        copy.start()
    f_in.start()
    c_in.start()
    for copy in rims_in[3:]:
        copy.start()
    for k in range(KERNELS):
        coef_in(k).start()
    a_in.start()
    b_in.start()

    for r in (rb, rb2):
        r[:, :, 0:TOP, :] = jnp.zeros((2, BLOCKS, TOP, 128), BF16)
        r[:, :, TOP + LAT :, :] = jnp.zeros((2, BLOCKS, RBR - LAT - TOP, 128), BF16)
    for r in (w, w2):
        r[:, :, EXT:, :] = jnp.zeros((2, BLOCKS, WR - EXT, 128), BF16)
    acc[...] = jnp.zeros_like(acc)
    none = jnp.zeros((FULL - REST, COLS), F32)
    for k in range(PLANES):
        plane, at = PLANES + REST * k // FULL, REST * k % FULL
        near_rest = near_ref[plane].astype(F32)[at : at + REST]
        far_rest = far_ref[plane].astype(F32)[at : at + REST]
        rest_above = jnp.where(even > 0, far_rest, near_rest)
        rest_below = jnp.where(even > 0, near_rest, far_rest)
        tile_above = jnp.concatenate([none, rest_above], axis=0).astype(BF16)
        tile_below = jnp.concatenate([rest_below, none], axis=0).astype(BF16)
        if k < KERNELS:
            coef[k, 0:FULL, :] = tile_above
            coef[k, EXT - FULL :, :] = tile_below
        else:
            obs[0:FULL, :] = tile_above
            obs[EXT - FULL :, :] = tile_below
    low = lax.broadcasted_iota(jnp.int32, (LAT, 128), 1) < 64
    for j in range(BLOCKS):
        own, edges = [], []
        for e in range(4 * j, 4 * j + 4):
            own.append(strip_ref[e, 0:OWN, :].astype(F32))
            edge = strip_ref[e, OWN:, :].astype(F32)
            edges += [edge[:, 64 * g : 64 * g + 64] for g in range(OWN // EDGE)]
        edges = jnp.concatenate(edges, axis=0).T
        sky[j, 0:SKY, :] = edges[0:SKY]
        sky[j, SKY : SKY + ROWS, :] = jnp.concatenate(own, axis=0).T
        sky[j, SKY + ROWS :, :] = edges[SKY : 2 * SKY]
    zero = jnp.zeros((LAT, 128), F32)
    for j in range(BLOCKS):
        after = sky[j + 1] if j + 1 < BLOCKS else zero
        before = sky[j - 1] if j > 0 else zero
        windows[j, :, 0:128] = sky[j].astype(BF16)
        windows[j, :, 128:256] = jnp.where(low, after, before).astype(BF16)
    for copy in rims_in[:3]:
        copy.wait()
    pred[...] = -obs[...].astype(F32)
    for copy in rims_in[3:]:
        copy.wait()
    f_in.wait()
    c_in.wait()

    def blur(i, rb):
        f = f_ref[i]
        for j in range(BLOCKS):
            both = dot(windows[j], f)
            rb[0, j, TOP : TOP + LAT, :] = both[:, :128].astype(BF16)
            rb[1, j, TOP : TOP + LAT, :] = both[:, 128:].astype(BF16)

    def predict(i, rb):
        for q in range(2):
            k = 2 * i + q
            c = c_ref[k]
            for h in range(2):
                out = slice(HOUT * h, HOUT * h + HOUT)
                for x in range(0, BLOCKS, 2):
                    at = slice(HOUT * h, HOUT * h + 256)
                    v = dot(c, jnp.concatenate([rb[q, x, at, :], rb[q, x + 1, at, :]], axis=1))
                    cols = slice(128 * x, 128 * x + 256)
                    pred[out, cols] += coef[k, out, cols].astype(F32) * v

    def forward(n, carry):
        for m in range(4):
            coef_in(4 * n + m).wait()
        blur(2 * n, rb)
        blur(2 * n + 1, rb2)
        predict(2 * n, rb)
        predict(2 * n + 1, rb2)
        return carry

    lax.fori_loop(0, PAIRS // 2, forward, 0)

    mask = column_of(valid_ref[...].astype(F32))
    for j in range(BLOCKS):
        pred[RIM : RIM + ROWS, 128 * j : 128 * j + 128] *= mask
    res_out = pltpu.make_async_copy(pred.at[pl.ds(RIM, ROWS), :], res_hbm.at[0], rim_sem.at[0])
    res_out.start()

    low_y = lax.broadcasted_iota(jnp.int32, (ROWS, 128), 1) < 64
    none = jnp.zeros((ROWS, 128), BF16)

    def weigh(i, w):
        for q in range(2):
            for x in range(BLOCKS):
                cols = slice(128 * x, 128 * x + 128)
                w[q, x, 0:EXT, :] = (coef[2 * i + q, :, cols].astype(F32) * pred[:, cols]).astype(BF16)

    def back(i, w, cb):
        for q in range(2):
            a = a_ref[2 * i + q]
            for h in range(2):
                for x in range(0, BLOCKS, 2):
                    at = slice(128 * h, 128 * h + 256)
                    both = dot(a, jnp.concatenate([w[q, x, at, :], w[q, x + 1, at, :]], axis=1))
                    cb[q, x, 128 * h : 128 * h + 128, :] = both[:, :128].astype(BF16)
                    cb[q, x + 1, 128 * h : 128 * h + 128, :] = both[:, 128:].astype(BF16)
        b = b_ref[i]
        for x in range(0, BLOCKS, 2):
            parts = [cb[0, x], cb[0, x + 1], cb[1, x], cb[1, x + 1]]
            for q in range(2):
                after = cb[q, x + 2] if x + 2 < BLOCKS else none
                before = cb[q, x - 1] if x > 0 else none
                parts.append(jnp.where(low_y, after, before))
            acc[x // 2] += dot(jnp.concatenate(parts, axis=1), b)

    weigh(0, w)
    a_in.wait()
    b_in.wait()

    def adjoint(n, carry):
        weigh(2 * n + 1, w2)
        back(2 * n, w, cb)
        weigh(jnp.minimum(2 * n + 2, PAIRS - 1), w)
        back(2 * n + 1, w2, cb2)
        return carry

    lax.fori_loop(0, PAIRS // 2, adjoint, 0)
    for x in range(BLOCKS // 2):
        send_ref[256 * x : 256 * x + 256, :] = acc[x].T.astype(BF16)
    res_out.wait()


def main(even, strip, valid, bands, coefficients, observed, near, far):
    return pl.pallas_call(
        main_kernel,
        out_shape=(
            jax.ShapeDtypeStruct((1, ROWS, COLS), F32),
            jax.ShapeDtypeStruct((COLS, ROWS), BF16),
        ),
        in_specs=[SMEM] + [VMEM] * 2 + [HBM] * 6 + [VMEM] * 2,
        out_specs=(ANY, VMEM),
        scratch_shapes=[
            pltpu.VMEM((PAIRS, 256, 256), BF16),
            pltpu.VMEM((KERNELS, HOUT, 256), BF16),
            pltpu.VMEM((KERNELS, 128, 256), BF16),
            pltpu.VMEM((PAIRS, 768, 256), BF16),
            pltpu.VMEM((BLOCKS, LAT, 128), F32),
            pltpu.VMEM((BLOCKS, LAT, 256), BF16),
            pltpu.VMEM((KERNELS, EXT, COLS), BF16),
            pltpu.VMEM((EXT, COLS), BF16),
            pltpu.VMEM((2, BLOCKS, RBR, 128), BF16),
            pltpu.VMEM((2, BLOCKS, RBR, 128), BF16),
            pltpu.VMEM((EXT, COLS), F32),
            pltpu.VMEM((2, BLOCKS, WR, 128), BF16),
            pltpu.VMEM((2, BLOCKS, WR, 128), BF16),
            pltpu.VMEM((2, BLOCKS, ROWS, 128), BF16),
            pltpu.VMEM((2, BLOCKS, ROWS, 128), BF16),
            pltpu.VMEM((BLOCKS // 2, ROWS, 256), F32),
            pltpu.SemaphoreType.DMA((KERNELS,)),
            pltpu.SemaphoreType.DMA((5,)),
            pltpu.SemaphoreType.DMA((4,)),
        ],
        compiler_params=pltpu.CompilerParams(vmem_limit_bytes=56 << 20),
        name="main",
    )(even, strip, valid, *bands, coefficients, observed, near, far)


def gather_kernel(cell_ref, terms_ref, out_ref):
    out_ref[...] = jnp.zeros_like(out_ref)
    for e in range(EXPOSURES):
        out_ref[cell_ref[0, e]] += terms_ref[e].astype(F32)


def gather(cell_of, terms):
    return pl.pallas_call(
        gather_kernel,
        out_shape=jax.ShapeDtypeStruct((CELLS, OWN, ROWS), F32),
        in_specs=[SMEM, VMEM],
        out_specs=VMEM,
        name="gather",
    )(cell_of, terms)


def keep(*arrays):
    return [pltpu.with_memory_space_constraint(a, pltpu.VMEM) for a in arrays]


def body(latent, row_taps, column_taps, coefficients, observed, cell_of, valid_rows):
    count = lax.axis_size("row")
    even = 1 - lax.rem(lax.axis_index("row"), 2)
    chip = [(i, i ^ 1) for i in range(count)]
    across = [(i, i + 1) for i in range(1, count - 1, 2)] + [(i + 1, i) for i in range(1, count - 1, 2)]
    cell_of = cell_of.reshape(1, EXPOSURES)
    latent = jnp.swapaxes(latent, 1, 2)

    even = even.reshape(1, 1)
    far_sky = lax.ppermute(latent, "row", across)
    near_sky = lax.ppermute(latent, "row", chip)
    near_rim, far_rim = cut(even, valid_rows, observed, coefficients)
    packed = pack(even, cell_of, latent, *keep(near_sky, far_sky))
    strip = lax.all_to_all(packed, "exp", 0, 0, tiled=True)
    far_rim = lax.ppermute(far_rim, "row", across)
    near_rim = lax.ppermute(near_rim, "row", chip)
    f, c, a, b = make_bands(row_taps, column_taps)
    residual, send = main(
        even, *keep(strip), valid_rows, (f, c, a, b), coefficients, observed, *keep(near_rim, far_rim)
    )
    terms = lax.all_to_all(send.reshape(EXPOSURES, OWN, ROWS), "exp", 0, 0, tiled=True)
    return jnp.swapaxes(gather(cell_of, *keep(terms)), 1, 2), residual


def solution(mesh):
    placed = (
        P(None, "row", "exp"),
        P(),
        P(),
        P("exp", None, "row", None),
        P("exp", "row", None),
        P(),
        P("exp", "row"),
    )
    return jax.shard_map(
        body,
        mesh=mesh,
        in_specs=placed,
        out_specs=(P(None, "row", "exp"), P("exp", "row", None)),
        check_vma=False,
    )
```

```python
import jax
import jax.numpy as jnp
from jax import lax
from jax.experimental import pallas as pl
from jax.experimental.pallas import tpu as pltpu
from jax.sharding import PartitionSpec as P


F32 = jnp.float32
BF16 = jnp.bfloat16
KERNELS = 16
PAIRS = KERNELS // 2
TAPS = 21
HALF = TAPS // 2
CELLS = 4
EXPOSURES = 32
ROWS = 256
COLS = 1024
BLOCKS = COLS // 128
OWN = COLS // EXPOSURES
SKY = 24
RIM = 16
FULL = 8
REST = HALF - FULL
PLANES = KERNELS + 1
LAT = ROWS + 2 * SKY
EDGE = 8
EXT = ROWS + 2 * RIM
HOUT = EXT // 2
TOP = 8
RBR = HOUT + 256
WR = 384

VMEM = pl.BlockSpec(memory_space=pltpu.VMEM)
SMEM = pl.BlockSpec(memory_space=pltpu.SMEM)
ANY = pl.BlockSpec(memory_space=pl.ANY)
HBM = pl.BlockSpec(memory_space=pltpu.HBM)


def dot(a, b):
    return lax.dot_general(a, b, (((1,), (0,)), ((), ())), preferred_element_type=F32)


def column_of(valid):
    return jnp.broadcast_to(valid, (128, valid.shape[1])).T


def cut_kernel(even_ref, valid_ref, obs_hbm, coef_hbm, near_ref, far_ref, near_in, far_in, sem):
    even = even_ref[0, 0]
    outs = ((even, near_ref, near_in), (1 - even, far_ref, far_in))
    copies = []
    for n, (last, _, block) in enumerate(outs):
        rows = pl.ds(pl.multiple_of(last * (ROWS - RIM), RIM), RIM)
        copies += [
            pltpu.make_async_copy(coef_hbm.at[0, :, rows, :], block.at[pl.ds(0, KERNELS)], sem.at[2 * n]),
            pltpu.make_async_copy(obs_hbm.at[0, rows, :], block.at[KERNELS], sem.at[2 * n + 1]),
        ]
    for copy in copies:
        copy.start()
    mask = column_of(valid_ref[...].astype(F32))
    head_mask = jnp.concatenate([mask[:RIM]] * BLOCKS, axis=1)
    tail_mask = jnp.concatenate([mask[ROWS - RIM :]] * BLOCKS, axis=1)
    for copy in copies:
        copy.wait()
    for last, out, block in outs:
        tail = last > 0
        usable = jnp.where(tail, tail_mask, head_mask)
        rest = []
        for k in range(PLANES):
            rows = block[k].astype(F32) * usable
            out[k] = jnp.where(tail, rows[RIM - FULL :], rows[:FULL]).astype(BF16)
            rest.append(jnp.where(tail, rows[RIM - HALF : RIM - FULL], rows[FULL:HALF]))
        rest += [jnp.zeros((REST, COLS), F32)] * (-PLANES * REST % FULL // REST)
        for n in range(len(rest) * REST // FULL):
            each = FULL // REST
            out[PLANES + n] = jnp.concatenate(rest[each * n : each * n + each], axis=0).astype(BF16)


def cut(even, valid, observed, coefficients):
    planes = PLANES + -(-PLANES * REST // FULL)
    block = pltpu.VMEM((PLANES, RIM, COLS), BF16)
    return pl.pallas_call(
        cut_kernel,
        out_shape=(jax.ShapeDtypeStruct((planes, FULL, COLS), BF16),) * 2,
        in_specs=[SMEM, VMEM, HBM, HBM],
        out_specs=(VMEM,) * 2,
        scratch_shapes=[block, block, pltpu.SemaphoreType.DMA((4,))],
        name="cut",
    )(even, valid, observed, coefficients)


def pack_kernel(even_ref, cell_ref, lat_ref, near_ref, far_ref, out_ref, turned):
    even = even_ref[0, 0] > 0
    fill = jnp.zeros((OWN, 64 - 2 * SKY), F32)
    for c in range(CELLS):
        near, far = near_ref[c].astype(F32), far_ref[c].astype(F32)
        above = jnp.where(even, far[:, ROWS - SKY :], near[:, ROWS - SKY :])
        below = jnp.where(even, near[:, :SKY], far[:, :SKY])
        edges = jnp.concatenate([above, below, fill], axis=1)
        turned[c, 0:OWN, :] = lat_ref[c]
        turned[c, OWN:, :] = jnp.concatenate(
            [edges[EDGE * g : EDGE * g + EDGE] for g in range(OWN // EDGE)], axis=1
        ).astype(BF16)
    for e in range(EXPOSURES):
        out_ref[e] = turned[cell_ref[0, e]]


def pack(even, cell_of, latent, near, far):
    return pl.pallas_call(
        pack_kernel,
        out_shape=jax.ShapeDtypeStruct((EXPOSURES, OWN + EDGE, ROWS), BF16),
        in_specs=[SMEM, SMEM, VMEM, VMEM, VMEM],
        out_specs=VMEM,
        scratch_shapes=[pltpu.VMEM((CELLS, OWN + EDGE, ROWS), BF16)],
        name="pack",
    )(even, cell_of, latent, near, far)


def base_rows(taps, place):
    lane = lax.broadcasted_iota(jnp.int32, (KERNELS, 256), 1)
    out = jnp.zeros((KERNELS, 256), F32)
    for t in range(TAPS):
        out = jnp.where(lane == place(t) % 256, taps[:, t : t + 1], out)
    return out


def skewed(row, count):
    return pltpu.roll(jnp.broadcast_to(row, (count, 256)), 0, 1, stride=1, stride_axis=0)


def bands_kernel(row_ref, col_ref, f_ref, c_hbm, a_hbm, b_hbm, c_ref, a_ref, b_ref, sem):
    c_out = pltpu.make_async_copy(c_ref, c_hbm, sem.at[PAIRS + 1])
    a_out = pltpu.make_async_copy(a_ref, a_hbm, sem.at[PAIRS])
    b_out = [pltpu.make_async_copy(b_ref.at[i], b_hbm.at[i], sem.at[i]) for i in range(PAIRS)]
    rows = row_ref[...].astype(F32)
    cols = col_ref[...].astype(F32)
    f_base = base_rows(rows, lambda t: HALF - t)
    b_base = base_rows(rows, lambda t: t - HALF)
    c_base = base_rows(cols, lambda t: t + 2 * RIM - RIM - HALF)
    a_base = base_rows(cols, lambda t: RIM + HALF - t)
    at = lax.broadcasted_iota(jnp.int32, (256, 256), 0)
    out = lax.broadcasted_iota(jnp.int32, (256, 256), 1)
    near = jnp.abs(at - out) < 128
    for k in range(KERNELS):
        i, q = k // 2, k % 2
        f_ref[i, :, 128 * q : 128 * q + 128] = skewed(f_base[k : k + 1], 256)[:, :128].astype(BF16)
        b = skewed(b_base[k : k + 1], 256)
        b_ref[i, 256 * q : 256 * q + 256, :] = jnp.where(near, b, 0.0).astype(BF16)
        far = jnp.where(near, 0.0, b).astype(BF16)
        b_ref[i, 512 + 128 * q : 576 + 128 * q, :] = far[:64]
        b_ref[i, 576 + 128 * q : 640 + 128 * q, :] = far[192:]
        c_ref[k] = skewed(c_base[k : k + 1], HOUT).astype(BF16)
        a_ref[k] = skewed(a_base[k : k + 1], 128).astype(BF16)
        if q == 1:
            b_out[i].start()
    c_out.start()
    a_out.start()
    for copy in (*b_out, c_out, a_out):
        copy.wait()


def make_bands(row_taps, column_taps):
    return pl.pallas_call(
        bands_kernel,
        out_shape=(
            jax.ShapeDtypeStruct((PAIRS, 256, 256), BF16),
            jax.ShapeDtypeStruct((KERNELS, HOUT, 256), BF16),
            jax.ShapeDtypeStruct((KERNELS, 128, 256), BF16),
            jax.ShapeDtypeStruct((PAIRS, 768, 256), BF16),
        ),
        in_specs=[VMEM, VMEM],
        out_specs=(VMEM, HBM, HBM, HBM),
        scratch_shapes=[
            pltpu.VMEM((KERNELS, HOUT, 256), BF16),
            pltpu.VMEM((KERNELS, 128, 256), BF16),
            pltpu.VMEM((PAIRS, 768, 256), BF16),
            pltpu.SemaphoreType.DMA((PAIRS + 2,)),
        ],
        compiler_params=pltpu.CompilerParams(vmem_limit_bytes=56 << 20),
        name="bands",
    )(row_taps, column_taps)


def main_kernel(
    even_ref, strip_ref, valid_ref, f_hbm, c_hbm, a_hbm, b_hbm, coef_hbm, obs_hbm, near_ref, far_ref,
    res_hbm, send_ref,
    f_ref, c_ref, a_ref, b_ref, sky, windows, coef, obs, rb, rb2, pred, w, w2, cb, cb2, acc, sem, rim_sem, band_sem,
):
    def coef_in(k):
        return pltpu.make_async_copy(coef_hbm.at[0, k], coef.at[k, pl.ds(RIM, ROWS), :], sem.at[k])

    even = even_ref[0, 0]
    near_at = pl.ds(pl.multiple_of(FULL + even * (FULL + ROWS), FULL), FULL)
    far_at = pl.ds(pl.multiple_of(FULL + (1 - even) * (FULL + ROWS), FULL), FULL)
    rims_in = [
        pltpu.make_async_copy(obs_hbm.at[0], obs.at[pl.ds(RIM, ROWS), :], rim_sem.at[0]),
        pltpu.make_async_copy(near_ref.at[KERNELS], obs.at[near_at, :], rim_sem.at[1]),
        pltpu.make_async_copy(far_ref.at[KERNELS], obs.at[far_at, :], rim_sem.at[2]),
        pltpu.make_async_copy(near_ref.at[pl.ds(0, KERNELS)], coef.at[:, near_at, :], rim_sem.at[3]),
        pltpu.make_async_copy(far_ref.at[pl.ds(0, KERNELS)], coef.at[:, far_at, :], rim_sem.at[4]),
    ]
    f_in = pltpu.make_async_copy(f_hbm, f_ref, band_sem.at[3])
    c_in = pltpu.make_async_copy(c_hbm, c_ref, band_sem.at[2])
    a_in = pltpu.make_async_copy(a_hbm, a_ref, band_sem.at[0])
    b_in = pltpu.make_async_copy(b_hbm, b_ref, band_sem.at[1])
    f_in.start()
    for copy in rims_in[:3]:
        copy.start()
    c_in.start()
    for copy in rims_in[3:]:
        copy.start()
    for k in range(KERNELS):
        coef_in(k).start()
    a_in.start()
    b_in.start()

    for r in (rb, rb2):
        r[:, :, 0:TOP, :] = jnp.zeros((2, BLOCKS, TOP, 128), BF16)
        r[:, :, TOP + LAT :, :] = jnp.zeros((2, BLOCKS, RBR - LAT - TOP, 128), BF16)
    for r in (w, w2):
        r[:, :, EXT:, :] = jnp.zeros((2, BLOCKS, WR - EXT, 128), BF16)
    acc[...] = jnp.zeros_like(acc)
    none = jnp.zeros((FULL - REST, COLS), F32)
    for k in range(PLANES):
        plane, at = PLANES + REST * k // FULL, REST * k % FULL
        near_rest = near_ref[plane].astype(F32)[at : at + REST]
        far_rest = far_ref[plane].astype(F32)[at : at + REST]
        rest_above = jnp.where(even > 0, far_rest, near_rest)
        rest_below = jnp.where(even > 0, near_rest, far_rest)
        tile_above = jnp.concatenate([none, rest_above], axis=0).astype(BF16)
        tile_below = jnp.concatenate([rest_below, none], axis=0).astype(BF16)
        if k < KERNELS:
            coef[k, 0:FULL, :] = tile_above
            coef[k, EXT - FULL :, :] = tile_below
        else:
            obs[0:FULL, :] = tile_above
            obs[EXT - FULL :, :] = tile_below
    low = lax.broadcasted_iota(jnp.int32, (LAT, 128), 1) < 64
    for j in range(BLOCKS):
        own, edges = [], []
        for e in range(4 * j, 4 * j + 4):
            own.append(strip_ref[e, 0:OWN, :].astype(F32))
            edge = strip_ref[e, OWN:, :].astype(F32)
            edges += [edge[:, 64 * g : 64 * g + 64] for g in range(OWN // EDGE)]
        edges = jnp.concatenate(edges, axis=0).T
        sky[j, 0:SKY, :] = edges[0:SKY]
        sky[j, SKY : SKY + ROWS, :] = jnp.concatenate(own, axis=0).T
        sky[j, SKY + ROWS :, :] = edges[SKY : 2 * SKY]
    zero = jnp.zeros((LAT, 128), F32)
    for j in range(BLOCKS):
        after = sky[j + 1] if j + 1 < BLOCKS else zero
        before = sky[j - 1] if j > 0 else zero
        windows[j, :, 0:128] = sky[j].astype(BF16)
        windows[j, :, 128:256] = jnp.where(low, after, before).astype(BF16)

    def blur(i, rb):
        f = f_ref[i]
        for j in range(BLOCKS):
            both = dot(windows[j], f)
            rb[0, j, TOP : TOP + LAT, :] = both[:, :128].astype(BF16)
            rb[1, j, TOP : TOP + LAT, :] = both[:, 128:].astype(BF16)

    def predict(i, rb):
        for q in range(2):
            k = 2 * i + q
            c = c_ref[k]
            for h in range(2):
                out = slice(HOUT * h, HOUT * h + HOUT)
                for x in range(0, BLOCKS, 2):
                    at = slice(HOUT * h, HOUT * h + 256)
                    v = dot(c, jnp.concatenate([rb[q, x, at, :], rb[q, x + 1, at, :]], axis=1))
                    cols = slice(128 * x, 128 * x + 256)
                    pred[out, cols] += coef[k, out, cols].astype(F32) * v

    def forward(n, carry):
        for m in range(4):
            coef_in(4 * n + m).wait()
        blur(2 * n, rb)
        blur(2 * n + 1, rb2)
        predict(2 * n, rb)
        predict(2 * n + 1, rb2)
        return carry

    f_in.wait()
    blur(0, rb)
    blur(1, rb2)
    for copy in rims_in[:3]:
        copy.wait()
    pred[...] = -obs[...].astype(F32)
    for copy in rims_in[3:]:
        copy.wait()
    c_in.wait()
    for m in range(4):
        coef_in(m).wait()
    predict(0, rb)
    predict(1, rb2)
    lax.fori_loop(1, PAIRS // 2, forward, 0)

    mask = column_of(valid_ref[...].astype(F32))
    for j in range(BLOCKS):
        pred[RIM : RIM + ROWS, 128 * j : 128 * j + 128] *= mask
    res_out = pltpu.make_async_copy(pred.at[pl.ds(RIM, ROWS), :], res_hbm.at[0], rim_sem.at[0])
    res_out.start()

    low_y = lax.broadcasted_iota(jnp.int32, (ROWS, 128), 1) < 64
    none = jnp.zeros((ROWS, 128), BF16)

    def weigh(i, w):
        for q in range(2):
            for x in range(BLOCKS):
                cols = slice(128 * x, 128 * x + 128)
                w[q, x, 0:EXT, :] = (coef[2 * i + q, :, cols].astype(F32) * pred[:, cols]).astype(BF16)

    def back(i, w, cb):
        for q in range(2):
            a = a_ref[2 * i + q]
            for h in range(2):
                for x in range(0, BLOCKS, 2):
                    at = slice(128 * h, 128 * h + 256)
                    both = dot(a, jnp.concatenate([w[q, x, at, :], w[q, x + 1, at, :]], axis=1))
                    cb[q, x, 128 * h : 128 * h + 128, :] = both[:, :128].astype(BF16)
                    cb[q, x + 1, 128 * h : 128 * h + 128, :] = both[:, 128:].astype(BF16)
        b = b_ref[i]
        for x in range(0, BLOCKS, 2):
            parts = [cb[0, x], cb[0, x + 1], cb[1, x], cb[1, x + 1]]
            for q in range(2):
                after = cb[q, x + 2] if x + 2 < BLOCKS else none
                before = cb[q, x - 1] if x > 0 else none
                parts.append(jnp.where(low_y, after, before))
            acc[x // 2] += dot(jnp.concatenate(parts, axis=1), b)

    weigh(0, w)
    a_in.wait()
    b_in.wait()

    def adjoint(n, carry):
        weigh(2 * n + 1, w2)
        back(2 * n, w, cb)
        weigh(jnp.minimum(2 * n + 2, PAIRS - 1), w)
        back(2 * n + 1, w2, cb2)
        return carry

    lax.fori_loop(0, PAIRS // 2, adjoint, 0)
    for x in range(BLOCKS // 2):
        send_ref[256 * x : 256 * x + 256, :] = acc[x].T.astype(BF16)
    res_out.wait()


def main(even, strip, valid, bands, coefficients, observed, near, far):
    return pl.pallas_call(
        main_kernel,
        out_shape=(
            jax.ShapeDtypeStruct((1, ROWS, COLS), F32),
            jax.ShapeDtypeStruct((COLS, ROWS), BF16),
        ),
        in_specs=[SMEM] + [VMEM] * 2 + [HBM] * 6 + [VMEM] * 2,
        out_specs=(ANY, VMEM),
        scratch_shapes=[
            pltpu.VMEM((PAIRS, 256, 256), BF16),
            pltpu.VMEM((KERNELS, HOUT, 256), BF16),
            pltpu.VMEM((KERNELS, 128, 256), BF16),
            pltpu.VMEM((PAIRS, 768, 256), BF16),
            pltpu.VMEM((BLOCKS, LAT, 128), F32),
            pltpu.VMEM((BLOCKS, LAT, 256), BF16),
            pltpu.VMEM((KERNELS, EXT, COLS), BF16),
            pltpu.VMEM((EXT, COLS), BF16),
            pltpu.VMEM((2, BLOCKS, RBR, 128), BF16),
            pltpu.VMEM((2, BLOCKS, RBR, 128), BF16),
            pltpu.VMEM((EXT, COLS), F32),
            pltpu.VMEM((2, BLOCKS, WR, 128), BF16),
            pltpu.VMEM((2, BLOCKS, WR, 128), BF16),
            pltpu.VMEM((2, BLOCKS, ROWS, 128), BF16),
            pltpu.VMEM((2, BLOCKS, ROWS, 128), BF16),
            pltpu.VMEM((BLOCKS // 2, ROWS, 256), F32),
            pltpu.SemaphoreType.DMA((KERNELS,)),
            pltpu.SemaphoreType.DMA((5,)),
            pltpu.SemaphoreType.DMA((4,)),
        ],
        compiler_params=pltpu.CompilerParams(vmem_limit_bytes=56 << 20),
        name="main",
    )(even, strip, valid, *bands, coefficients, observed, near, far)


def gather_kernel(cell_ref, terms_ref, out_ref):
    out_ref[...] = jnp.zeros_like(out_ref)
    for e in range(EXPOSURES):
        out_ref[cell_ref[0, e]] += terms_ref[e].astype(F32)


def gather(cell_of, terms):
    return pl.pallas_call(
        gather_kernel,
        out_shape=jax.ShapeDtypeStruct((CELLS, OWN, ROWS), F32),
        in_specs=[SMEM, VMEM],
        out_specs=VMEM,
        name="gather",
    )(cell_of, terms)


def keep(*arrays):
    return [pltpu.with_memory_space_constraint(a, pltpu.VMEM) for a in arrays]


def body(latent, row_taps, column_taps, coefficients, observed, cell_of, valid_rows):
    count = lax.axis_size("row")
    even = 1 - lax.rem(lax.axis_index("row"), 2)
    chip = [(i, i ^ 1) for i in range(count)]
    across = [(i, i + 1) for i in range(1, count - 1, 2)] + [(i + 1, i) for i in range(1, count - 1, 2)]
    cell_of = cell_of.reshape(1, EXPOSURES)
    latent = jnp.swapaxes(latent, 1, 2)

    even = even.reshape(1, 1)
    far_sky = lax.ppermute(latent, "row", across)
    near_sky = lax.ppermute(latent, "row", chip)
    near_rim, far_rim = cut(even, valid_rows, observed, coefficients)
    packed = pack(even, cell_of, latent, *keep(near_sky, far_sky))
    strip = lax.all_to_all(packed, "exp", 0, 0, tiled=True)
    far_rim = lax.ppermute(far_rim, "row", across)
    near_rim = lax.ppermute(near_rim, "row", chip)
    f, c, a, b = make_bands(row_taps, column_taps)
    residual, send = main(
        even, *keep(strip), valid_rows, (f, c, a, b), coefficients, observed, *keep(near_rim, far_rim)
    )
    terms = lax.all_to_all(send.reshape(EXPOSURES, OWN, ROWS), "exp", 0, 0, tiled=True)
    return jnp.swapaxes(gather(cell_of, *keep(terms)), 1, 2), residual


def solution(mesh):
    placed = (
        P(None, "row", "exp"),
        P(),
        P(),
        P("exp", None, "row", None),
        P("exp", "row", None),
        P(),
        P("exp", "row"),
    )
    return jax.shard_map(
        body,
        mesh=mesh,
        in_specs=placed,
        out_specs=(P(None, "row", "exp"), P("exp", "row", None)),
        check_vma=False,
    )
```

```python
import jax
import jax.numpy as jnp
from jax import lax
from jax.experimental import pallas as pl
from jax.experimental.pallas import tpu as pltpu
from jax.sharding import PartitionSpec as P


F32 = jnp.float32
BF16 = jnp.bfloat16
KERNELS = 16
PAIRS = KERNELS // 2
TAPS = 21
HALF = TAPS // 2
CELLS = 4
EXPOSURES = 32
ROWS = 256
COLS = 1024
BLOCKS = COLS // 128
OWN = COLS // EXPOSURES
SKY = 24
RIM = 16
FULL = 8
REST = HALF - FULL
PLANES = KERNELS + 1
LAT = ROWS + 2 * SKY
EDGE = 8
EXT = ROWS + 2 * RIM
HOUT = EXT // 2
TOP = 8
RBR = HOUT + 256
WR = 384

VMEM = pl.BlockSpec(memory_space=pltpu.VMEM)
SMEM = pl.BlockSpec(memory_space=pltpu.SMEM)
ANY = pl.BlockSpec(memory_space=pl.ANY)
HBM = pl.BlockSpec(memory_space=pltpu.HBM)


def dot(a, b):
    return lax.dot_general(a, b, (((1,), (0,)), ((), ())), preferred_element_type=F32)


def column_of(valid):
    return jnp.broadcast_to(valid, (128, valid.shape[1])).T


def cut_kernel(even_ref, valid_ref, obs_hbm, coef_hbm, near_hbm, far_hbm, blocks, made, sem, out_sem):
    even = even_ref[0, 0]
    lasts = (1 - even, even)
    copies, outs = [], []
    for n, (last, target) in enumerate(zip(lasts, (far_hbm, near_hbm))):
        rows = pl.ds(pl.multiple_of(last * (ROWS - RIM), RIM), RIM)
        copies.append(
            [
                pltpu.make_async_copy(
                    coef_hbm.at[0, :, rows, :], blocks.at[n, pl.ds(0, KERNELS)], sem.at[2 * n]
                ),
                pltpu.make_async_copy(obs_hbm.at[0, rows, :], blocks.at[n, KERNELS], sem.at[2 * n + 1]),
            ]
        )
        outs.append(pltpu.make_async_copy(made.at[n], target, out_sem.at[n]))
    for copy in copies[0] + copies[1]:
        copy.start()
    mask = column_of(valid_ref[...].astype(F32))
    head_mask = jnp.concatenate([mask[:RIM]] * BLOCKS, axis=1)
    tail_mask = jnp.concatenate([mask[ROWS - RIM :]] * BLOCKS, axis=1)
    for n, last in enumerate(lasts):
        for copy in copies[n]:
            copy.wait()
        tail = last > 0
        usable = jnp.where(tail, tail_mask, head_mask)
        rest = []
        for k in range(PLANES):
            rows = blocks[n, k].astype(F32) * usable
            made[n, k] = jnp.where(tail, rows[RIM - FULL :], rows[:FULL]).astype(BF16)
            rest.append(jnp.where(tail, rows[RIM - HALF : RIM - FULL], rows[FULL:HALF]))
        rest += [jnp.zeros((REST, COLS), F32)] * (-PLANES * REST % FULL // REST)
        for m in range(len(rest) * REST // FULL):
            each = FULL // REST
            made[n, PLANES + m] = jnp.concatenate(rest[each * m : each * m + each], axis=0).astype(BF16)
        outs[n].start()
    for copy in outs:
        copy.wait()


def cut(even, valid, observed, coefficients):
    planes = PLANES + -(-PLANES * REST // FULL)
    return pl.pallas_call(
        cut_kernel,
        out_shape=(jax.ShapeDtypeStruct((planes, FULL, COLS), BF16),) * 2,
        in_specs=[SMEM, VMEM, HBM, HBM],
        out_specs=(HBM,) * 2,
        scratch_shapes=[
            pltpu.VMEM((2, PLANES, RIM, COLS), BF16),
            pltpu.VMEM((2, planes, FULL, COLS), BF16),
            pltpu.SemaphoreType.DMA((4,)),
            pltpu.SemaphoreType.DMA((2,)),
        ],
        name="cut",
    )(even, valid, observed, coefficients)


def pack_kernel(even_ref, cell_ref, lat_ref, near_ref, far_ref, out_hbm, turned, sem):
    even = even_ref[0, 0] > 0
    fill = jnp.zeros((OWN, 64 - 2 * SKY), F32)
    for c in range(CELLS):
        near, far = near_ref[c].astype(F32), far_ref[c].astype(F32)
        above = jnp.where(even, far[:, ROWS - SKY :], near[:, ROWS - SKY :])
        below = jnp.where(even, near[:, :SKY], far[:, :SKY])
        edges = jnp.concatenate([above, below, fill], axis=1)
        turned[c, 0:OWN, :] = lat_ref[c]
        turned[c, OWN:, :] = jnp.concatenate(
            [edges[EDGE * g : EDGE * g + EDGE] for g in range(OWN // EDGE)], axis=1
        ).astype(BF16)
    copies = [
        pltpu.make_async_copy(turned.at[cell_ref[0, e]], out_hbm.at[e], sem.at[e]) for e in range(EXPOSURES)
    ]
    for copy in copies:
        copy.start()
    for copy in copies:
        copy.wait()


def pack(even, cell_of, latent, near, far):
    return pl.pallas_call(
        pack_kernel,
        out_shape=jax.ShapeDtypeStruct((EXPOSURES, OWN + EDGE, ROWS), BF16),
        in_specs=[SMEM, SMEM, VMEM, VMEM, VMEM],
        out_specs=HBM,
        scratch_shapes=[pltpu.VMEM((CELLS, OWN + EDGE, ROWS), BF16), pltpu.SemaphoreType.DMA((EXPOSURES,))],
        name="pack",
    )(even, cell_of, latent, near, far)


def base_rows(taps, place):
    lane = lax.broadcasted_iota(jnp.int32, (KERNELS, 256), 1)
    out = jnp.zeros((KERNELS, 256), F32)
    for t in range(TAPS):
        out = jnp.where(lane == place(t) % 256, taps[:, t : t + 1], out)
    return out


def skewed(row, count):
    return pltpu.roll(jnp.broadcast_to(row, (count, 256)), 0, 1, stride=1, stride_axis=0)


def bands_kernel(row_ref, col_ref, f_ref, c_hbm, a_hbm, b_hbm, c_ref, a_ref, b_ref, sem):
    c_out = pltpu.make_async_copy(c_ref, c_hbm, sem.at[PAIRS + 1])
    a_out = pltpu.make_async_copy(a_ref, a_hbm, sem.at[PAIRS])
    b_out = [pltpu.make_async_copy(b_ref.at[i], b_hbm.at[i], sem.at[i]) for i in range(PAIRS)]
    rows = row_ref[...].astype(F32)
    cols = col_ref[...].astype(F32)
    f_base = base_rows(rows, lambda t: HALF - t)
    b_base = base_rows(rows, lambda t: t - HALF)
    c_base = base_rows(cols, lambda t: t + 2 * RIM - RIM - HALF)
    a_base = base_rows(cols, lambda t: RIM + HALF - t)
    at = lax.broadcasted_iota(jnp.int32, (256, 256), 0)
    out = lax.broadcasted_iota(jnp.int32, (256, 256), 1)
    near = jnp.abs(at - out) < 128
    for k in range(KERNELS):
        i, q = k // 2, k % 2
        f_ref[i, :, 128 * q : 128 * q + 128] = skewed(f_base[k : k + 1], 256)[:, :128].astype(BF16)
        b = skewed(b_base[k : k + 1], 256)
        b_ref[i, 256 * q : 256 * q + 256, :] = jnp.where(near, b, 0.0).astype(BF16)
        far = jnp.where(near, 0.0, b).astype(BF16)
        b_ref[i, 512 + 128 * q : 576 + 128 * q, :] = far[:64]
        b_ref[i, 576 + 128 * q : 640 + 128 * q, :] = far[192:]
        c_ref[k] = skewed(c_base[k : k + 1], HOUT).astype(BF16)
        a_ref[k] = skewed(a_base[k : k + 1], 128).astype(BF16)
        if q == 1:
            b_out[i].start()
    c_out.start()
    a_out.start()
    for copy in (*b_out, c_out, a_out):
        copy.wait()


def make_bands(row_taps, column_taps):
    return pl.pallas_call(
        bands_kernel,
        out_shape=(
            jax.ShapeDtypeStruct((PAIRS, 256, 256), BF16),
            jax.ShapeDtypeStruct((KERNELS, HOUT, 256), BF16),
            jax.ShapeDtypeStruct((KERNELS, 128, 256), BF16),
            jax.ShapeDtypeStruct((PAIRS, 768, 256), BF16),
        ),
        in_specs=[VMEM, VMEM],
        out_specs=(VMEM, HBM, HBM, HBM),
        scratch_shapes=[
            pltpu.VMEM((KERNELS, HOUT, 256), BF16),
            pltpu.VMEM((KERNELS, 128, 256), BF16),
            pltpu.VMEM((PAIRS, 768, 256), BF16),
            pltpu.SemaphoreType.DMA((PAIRS + 2,)),
        ],
        compiler_params=pltpu.CompilerParams(vmem_limit_bytes=56 << 20),
        name="bands",
    )(row_taps, column_taps)


def main_kernel(
    even_ref, strip_ref, valid_ref, f_hbm, c_hbm, a_hbm, b_hbm, coef_hbm, obs_hbm, near_ref, far_ref,
    res_hbm, send_hbm,
    f_ref, c_ref, a_ref, b_ref, turned, sky, windows, coef, obs, rb, rb2, pred, w, w2, cb, cb2, acc, sem, rim_sem, band_sem,
):
    def coef_in(k):
        return pltpu.make_async_copy(coef_hbm.at[0, k], coef.at[k, pl.ds(RIM, ROWS), :], sem.at[k])

    even = even_ref[0, 0]
    near_at = pl.ds(pl.multiple_of(FULL + even * (FULL + ROWS), FULL), FULL)
    far_at = pl.ds(pl.multiple_of(FULL + (1 - even) * (FULL + ROWS), FULL), FULL)
    rims_in = [
        pltpu.make_async_copy(obs_hbm.at[0], obs.at[pl.ds(RIM, ROWS), :], rim_sem.at[0]),
        pltpu.make_async_copy(near_ref.at[KERNELS], obs.at[near_at, :], rim_sem.at[1]),
        pltpu.make_async_copy(far_ref.at[KERNELS], obs.at[far_at, :], rim_sem.at[2]),
        pltpu.make_async_copy(near_ref.at[pl.ds(0, KERNELS)], coef.at[:, near_at, :], rim_sem.at[3]),
        pltpu.make_async_copy(far_ref.at[pl.ds(0, KERNELS)], coef.at[:, far_at, :], rim_sem.at[4]),
    ]
    f_in = pltpu.make_async_copy(f_hbm, f_ref, band_sem.at[3])
    c_in = pltpu.make_async_copy(c_hbm, c_ref, band_sem.at[2])
    a_in = pltpu.make_async_copy(a_hbm, a_ref, band_sem.at[0])
    b_in = pltpu.make_async_copy(b_hbm, b_ref, band_sem.at[1])
    f_in.start()
    for copy in rims_in[:3]:
        copy.start()
    c_in.start()
    for copy in rims_in[3:]:
        copy.start()
    for k in range(KERNELS):
        coef_in(k).start()
    a_in.start()
    b_in.start()

    for r in (rb, rb2):
        r[:, :, 0:TOP, :] = jnp.zeros((2, BLOCKS, TOP, 128), BF16)
        r[:, :, TOP + LAT :, :] = jnp.zeros((2, BLOCKS, RBR - LAT - TOP, 128), BF16)
    for r in (w, w2):
        r[:, :, EXT:, :] = jnp.zeros((2, BLOCKS, WR - EXT, 128), BF16)
    acc[...] = jnp.zeros_like(acc)
    none = jnp.zeros((FULL - REST, COLS), F32)
    for k in range(PLANES):
        plane, at = PLANES + REST * k // FULL, REST * k % FULL
        near_rest = near_ref[plane].astype(F32)[at : at + REST]
        far_rest = far_ref[plane].astype(F32)[at : at + REST]
        rest_above = jnp.where(even > 0, far_rest, near_rest)
        rest_below = jnp.where(even > 0, near_rest, far_rest)
        tile_above = jnp.concatenate([none, rest_above], axis=0).astype(BF16)
        tile_below = jnp.concatenate([rest_below, none], axis=0).astype(BF16)
        if k < KERNELS:
            coef[k, 0:FULL, :] = tile_above
            coef[k, EXT - FULL :, :] = tile_below
        else:
            obs[0:FULL, :] = tile_above
            obs[EXT - FULL :, :] = tile_below
    low = lax.broadcasted_iota(jnp.int32, (LAT, 128), 1) < 64
    for j in range(BLOCKS):
        own, edges = [], []
        for e in range(4 * j, 4 * j + 4):
            own.append(strip_ref[e, 0:OWN, :].astype(F32))
            edge = strip_ref[e, OWN:, :].astype(F32)
            edges += [edge[:, 64 * g : 64 * g + 64] for g in range(OWN // EDGE)]
        edges = jnp.concatenate(edges, axis=0).T
        sky[j, 0:SKY, :] = edges[0:SKY]
        sky[j, SKY : SKY + ROWS, :] = jnp.concatenate(own, axis=0).T
        sky[j, SKY + ROWS :, :] = edges[SKY : 2 * SKY]
    zero = jnp.zeros((LAT, 128), F32)
    for j in range(BLOCKS):
        after = sky[j + 1] if j + 1 < BLOCKS else zero
        before = sky[j - 1] if j > 0 else zero
        windows[j, :, 0:128] = sky[j].astype(BF16)
        windows[j, :, 128:256] = jnp.where(low, after, before).astype(BF16)

    def blur(i, rb):
        f = f_ref[i]
        for j in range(BLOCKS):
            both = dot(windows[j], f)
            rb[0, j, TOP : TOP + LAT, :] = both[:, :128].astype(BF16)
            rb[1, j, TOP : TOP + LAT, :] = both[:, 128:].astype(BF16)

    def predict(i, rb):
        for q in range(2):
            k = 2 * i + q
            c = c_ref[k]
            for h in range(2):
                out = slice(HOUT * h, HOUT * h + HOUT)
                for x in range(0, BLOCKS, 2):
                    at = slice(HOUT * h, HOUT * h + 256)
                    v = dot(c, jnp.concatenate([rb[q, x, at, :], rb[q, x + 1, at, :]], axis=1))
                    cols = slice(128 * x, 128 * x + 256)
                    pred[out, cols] += coef[k, out, cols].astype(F32) * v

    def forward(n, carry):
        for m in range(4):
            coef_in(4 * n + m).wait()
        blur(2 * n, rb)
        blur(2 * n + 1, rb2)
        predict(2 * n, rb)
        predict(2 * n + 1, rb2)
        return carry

    f_in.wait()
    blur(0, rb)
    blur(1, rb2)
    for copy in rims_in[:3]:
        copy.wait()
    pred[...] = -obs[...].astype(F32)
    for copy in rims_in[3:]:
        copy.wait()
    c_in.wait()
    for m in range(4):
        coef_in(m).wait()
    predict(0, rb)
    predict(1, rb2)
    lax.fori_loop(1, PAIRS // 2, forward, 0)

    mask = column_of(valid_ref[...].astype(F32))
    for j in range(BLOCKS):
        pred[RIM : RIM + ROWS, 128 * j : 128 * j + 128] *= mask
    res_out = pltpu.make_async_copy(pred.at[pl.ds(RIM, ROWS), :], res_hbm.at[0], rim_sem.at[0])
    res_out.start()

    low_y = lax.broadcasted_iota(jnp.int32, (ROWS, 128), 1) < 64
    none = jnp.zeros((ROWS, 128), BF16)

    def weigh(i, w):
        for q in range(2):
            for x in range(BLOCKS):
                cols = slice(128 * x, 128 * x + 128)
                w[q, x, 0:EXT, :] = (coef[2 * i + q, :, cols].astype(F32) * pred[:, cols]).astype(BF16)

    def back(i, w, cb):
        for q in range(2):
            a = a_ref[2 * i + q]
            for h in range(2):
                for x in range(0, BLOCKS, 2):
                    at = slice(128 * h, 128 * h + 256)
                    both = dot(a, jnp.concatenate([w[q, x, at, :], w[q, x + 1, at, :]], axis=1))
                    cb[q, x, 128 * h : 128 * h + 128, :] = both[:, :128].astype(BF16)
                    cb[q, x + 1, 128 * h : 128 * h + 128, :] = both[:, 128:].astype(BF16)
        b = b_ref[i]
        for x in range(0, BLOCKS, 2):
            parts = [cb[0, x], cb[0, x + 1], cb[1, x], cb[1, x + 1]]
            for q in range(2):
                after = cb[q, x + 2] if x + 2 < BLOCKS else none
                before = cb[q, x - 1] if x > 0 else none
                parts.append(jnp.where(low_y, after, before))
            acc[x // 2] += dot(jnp.concatenate(parts, axis=1), b)

    weigh(0, w)
    a_in.wait()
    b_in.wait()

    def adjoint(n, carry):
        weigh(2 * n + 1, w2)
        back(2 * n, w, cb)
        weigh(jnp.minimum(2 * n + 2, PAIRS - 1), w)
        back(2 * n + 1, w2, cb2)
        return carry

    lax.fori_loop(0, PAIRS // 2, adjoint, 0)
    outs = []
    for x in range(BLOCKS // 2):
        at = pl.ds(256 * x, 256)
        turned[at, :] = acc[x].T.astype(BF16)
        outs.append(pltpu.make_async_copy(turned.at[at, :], send_hbm.at[at, :], rim_sem.at[1 + x]))
        outs[x].start()
    for copy in (*outs, res_out):
        copy.wait()


def main(even, strip, valid, bands, coefficients, observed, near, far):
    return pl.pallas_call(
        main_kernel,
        out_shape=(
            jax.ShapeDtypeStruct((1, ROWS, COLS), F32),
            jax.ShapeDtypeStruct((COLS, ROWS), BF16),
        ),
        in_specs=[SMEM] + [VMEM] * 2 + [HBM] * 6 + [VMEM] * 2,
        out_specs=(HBM, HBM),
        scratch_shapes=[
            pltpu.VMEM((PAIRS, 256, 256), BF16),
            pltpu.VMEM((KERNELS, HOUT, 256), BF16),
            pltpu.VMEM((KERNELS, 128, 256), BF16),
            pltpu.VMEM((PAIRS, 768, 256), BF16),
            pltpu.VMEM((COLS, ROWS), BF16),
            pltpu.VMEM((BLOCKS, LAT, 128), F32),
            pltpu.VMEM((BLOCKS, LAT, 256), BF16),
            pltpu.VMEM((KERNELS, EXT, COLS), BF16),
            pltpu.VMEM((EXT, COLS), BF16),
            pltpu.VMEM((2, BLOCKS, RBR, 128), BF16),
            pltpu.VMEM((2, BLOCKS, RBR, 128), BF16),
            pltpu.VMEM((EXT, COLS), F32),
            pltpu.VMEM((2, BLOCKS, WR, 128), BF16),
            pltpu.VMEM((2, BLOCKS, WR, 128), BF16),
            pltpu.VMEM((2, BLOCKS, ROWS, 128), BF16),
            pltpu.VMEM((2, BLOCKS, ROWS, 128), BF16),
            pltpu.VMEM((BLOCKS // 2, ROWS, 256), F32),
            pltpu.SemaphoreType.DMA((KERNELS,)),
            pltpu.SemaphoreType.DMA((5,)),
            pltpu.SemaphoreType.DMA((4,)),
        ],
        compiler_params=pltpu.CompilerParams(vmem_limit_bytes=56 << 20),
        name="main",
    )(even, strip, valid, *bands, coefficients, observed, near, far)


def gather_kernel(cell_ref, terms_ref, out_ref):
    out_ref[...] = jnp.zeros_like(out_ref)
    for e in range(EXPOSURES):
        out_ref[cell_ref[0, e]] += terms_ref[e].astype(F32)


def gather(cell_of, terms):
    return pl.pallas_call(
        gather_kernel,
        out_shape=jax.ShapeDtypeStruct((CELLS, OWN, ROWS), F32),
        in_specs=[SMEM, VMEM],
        out_specs=VMEM,
        name="gather",
    )(cell_of, terms)


def keep(*arrays):
    return [pltpu.with_memory_space_constraint(a, pltpu.VMEM) for a in arrays]


def body(latent, row_taps, column_taps, coefficients, observed, cell_of, valid_rows):
    count = lax.axis_size("row")
    even = 1 - lax.rem(lax.axis_index("row"), 2)
    chip = [(i, i ^ 1) for i in range(count)]
    across = [(i, i + 1) for i in range(1, count - 1, 2)] + [(i + 1, i) for i in range(1, count - 1, 2)]
    cell_of = cell_of.reshape(1, EXPOSURES)
    latent = jnp.swapaxes(latent, 1, 2)

    even = even.reshape(1, 1)
    far_sky = lax.ppermute(latent, "row", across)
    near_sky = lax.ppermute(latent, "row", chip)
    near_rim, far_rim = cut(even, valid_rows, observed, coefficients)
    packed = pack(even, cell_of, latent, *keep(near_sky, far_sky))
    strip = lax.all_to_all(packed, "exp", 0, 0, tiled=True)
    far_rim = lax.ppermute(far_rim, "row", across)
    near_rim = lax.ppermute(near_rim, "row", chip)
    f, c, a, b = make_bands(row_taps, column_taps)
    residual, send = main(
        even, *keep(strip), valid_rows, (f, c, a, b), coefficients, observed, *keep(near_rim, far_rim)
    )
    terms = lax.all_to_all(send.reshape(EXPOSURES, OWN, ROWS), "exp", 0, 0, tiled=True)
    return jnp.swapaxes(gather(cell_of, *keep(terms)), 1, 2), residual


def solution(mesh):
    placed = (
        P(None, "row", "exp"),
        P(),
        P(),
        P("exp", None, "row", None),
        P("exp", "row", None),
        P(),
        P("exp", "row"),
    )
    return jax.shard_map(
        body,
        mesh=mesh,
        in_specs=placed,
        out_specs=(P(None, "row", "exp"), P("exp", "row", None)),
        check_vma=False,
    )
```
